32 devices in a mesh: section: 2 (over core), dp: 4 (over y, x), tensor: 4 (over z).
Axes of the slice: x: 2, y: 2, z: 4, core: 2. Of those that a mesh axis runs over, the one named last changes fastest.
Arguments:
- section_input: bfloat16 [2, 512, 4096], P('section', 'dp'), may hold values from -60 to 60
- weights: bfloat16 [2, 4096, 4096], P('section', 'tensor', 'dp'), may hold values from -0.1875 to 0.1875
- gains: float32 [2, 4096], P('section'), may hold values from 0.1 to 1.9
- proj_seeds: int32 [2, 2], P('section'), may hold values from 0 to 99999
- out_grad: bfloat16 [512, 4096], P('dp'), may hold values from -0.75 to 0.75
- query_grads: bfloat16 [2, 256, 4096], P('section', 'dp', 'tensor'), may hold values from -0.017944336 to 0.017944336
Outputs:
- projected_grads: float32 [2, 2, 4096], P('section', None, 'tensor')
- scores: float32 [2, 256], P(None, 'dp')
The draws below stay inside these ranges and needn't reach their ends.
All inputs are finite; a program needn't handle non-finite values.
Results may differ from the reference program's by a relative error of at most 0.033.
Values may be sent and summed in bfloat16 or wider, within the bound.
A program may use at most 64 MiB of HBM per device.

```python
import math
import jax
import jax.numpy as jnp
from jax import lax

D = 4096
R = 64
SEQS = 2
LAYERS = 2
TOKENS = 512
SEQ_LEN = 256
QUERIES = 256
N_TENSOR = 4


def draw_section_input(key, part):
    key_values = jax.random.fold_in(key, 101)
    key_columns = jax.random.fold_in(key, 202)
    key_rows = jax.random.fold_in(key, 303)
    col_scale = jnp.exp(jax.random.uniform(key_columns, (LAYERS, 1, D), jnp.float32, 0.0, math.log(10.0)))
    row_scale = jnp.exp(jax.random.uniform(key_rows, (LAYERS, TOKENS, 1), jnp.float32, 0.0, math.log(3.0)))
    values = jax.random.normal(key_values, (LAYERS, TOKENS, D), jnp.float32) * col_scale
    values = values * row_scale
    return jnp.clip(values, -60.0, 60.0).astype(jnp.bfloat16)


def place_ends(entries, stream_key, low, top_value):
    extent = entries.shape
    place = [jax.random.randint(jax.random.fold_in(stream_key, axis), (), 0, extent[axis]) for axis in range(len(extent))]
    entries = entries.at[tuple(place)].set(low)
    longest = extent.index(max(extent))
    place[longest] = (place[longest] + 1) % extent[longest]
    return entries.at[tuple(place)].set(top_value)


def steps_of(rng, extent, shards, low, high):
    factor_of, own = 1.0, jax.random.fold_in(rng, 6)
    for axis_at, shards_of in shards:
        steps = jnp.exp(jax.random.uniform(jax.random.fold_in(own, axis_at), (shards_of,), jnp.float32, low / len(shards), high / len(shards)))
        factor_of = factor_of * jnp.repeat(steps, extent[axis_at] // shards_of).reshape([-1 if axis == axis_at else 1 for axis in range(len(extent))])
    return factor_of


def gaussian(own_key, shape, spread, reach, pieces=(), kind=jnp.bfloat16):
    factor_of = steps_of(own_key, shape, pieces, -0.22, 0.18) if pieces else 1.0
    array = jax.random.normal(own_key, shape, jnp.float32) * spread * factor_of
    return jnp.minimum(jnp.maximum(array, -reach), reach).astype(kind)


def setup_inputs(seed: int = 0) -> dict:
    streams_of = jax.random.split(jax.random.key(seed), 7)
    return {
        "section_input": draw_section_input(jax.random.fold_in(streams_of[6], 71), 0),
        "weights": gaussian(streams_of[1], (LAYERS, D, D), (D // 4) ** -0.5, 0.1875, ((0, 2), (1, 4), (2, 4))),
        "gains": jnp.clip(1.0 + 0.18 * jax.random.normal(streams_of[2], (LAYERS, D), jnp.float32), 0.1, 1.9),
        "proj_seeds": place_ends(jax.random.randint(streams_of[3], (LAYERS, 2), 0, 100000), jax.random.fold_in(streams_of[3], 1), 0, 99999).astype(jnp.int32),
        "out_grad": gaussian(streams_of[4], (TOKENS, D), 0.125, 0.75, ((0, 4),)),
        "query_grads": gaussian(streams_of[5], (LAYERS, QUERIES, R * R), 0.003, 0.017944336, ((0, 2), (1, 4), (2, 4))),
    }


eps = 1e-05

def sign_table(seed_value, row_count):
    row_index = lax.broadcasted_iota(jnp.int32, (row_count, R), 0)
    col_index = lax.broadcasted_iota(jnp.int32, (row_count, R), 1)
    mixing = row_index * 40503 + col_index * 9973 + seed_value.astype(jnp.int32) * 7919 + 12345
    mixing = mixing ^ mixing >> 13
    mixing = mixing * 1274126177
    mixing = mixing ^ mixing >> 16
    parity = mixing >> 10 & 1
    return (jnp.where(parity == 1, 1.0, -1.0) * (1.0 / math.sqrt(row_count))).astype(jnp.bfloat16)

def silu_slope(values):
    sigmoid_v = jax.nn.sigmoid(values)
    return sigmoid_v * (1.0 + values * (1.0 - sigmoid_v))

def reference(section_input, weights, gains, proj_seeds, out_grad, query_grads):

    def layer_step(upstream, layer):
        layer_input, weight, gain_row, seed_pair, queries = layer
        hidden_in = layer_input.astype(jnp.float32)
        radius = jnp.sqrt(lax.optimization_barrier(jnp.mean(hidden_in * hidden_in, axis=1, keepdims=True)) + eps)
        normed = hidden_in / radius
        lifted = (normed * gain_row).astype(jnp.bfloat16)
        block_width = D // N_TENSOR
        summed = jnp.zeros((TOKENS, D), jnp.float32)
        for part_index in range(N_TENSOR):
            low_col = part_index * block_width
            partial_value = jnp.dot(lifted[:, low_col:low_col + block_width], weight[low_col:low_col + block_width, :], preferred_element_type=jnp.float32)
            summed = summed + lax.optimization_barrier(partial_value.astype(jnp.bfloat16)).astype(jnp.float32)
        proj_in = sign_table(seed_pair[0], D)
        proj_out = sign_table(seed_pair[1], D)
        in_features = jnp.dot(lifted, proj_in, preferred_element_type=jnp.float32).astype(jnp.bfloat16)
        grad_pre = (upstream.astype(jnp.float32) * silu_slope(summed)).astype(jnp.bfloat16)
        out_features = jnp.dot(grad_pre, proj_out, preferred_element_type=jnp.float32).astype(jnp.bfloat16)
        grad_norm = jnp.dot(grad_pre, weight.T, preferred_element_type=jnp.float32).astype(jnp.bfloat16)
        scaled = grad_norm.astype(jnp.float32) * gain_row
        mean_dot = lax.optimization_barrier(jnp.mean(scaled * normed, axis=1, keepdims=True))
        downstream = (upstream.astype(jnp.float32) + (scaled - normed * mean_dot) / radius).astype(jnp.bfloat16)
        left = in_features.astype(jnp.float32).reshape(SEQS, SEQ_LEN, R)
        right = out_features.astype(jnp.float32).reshape(SEQS, SEQ_LEN, R)
        grads = jnp.einsum('kti,ktj->kij', left, right, precision=lax.Precision.HIGHEST).reshape(SEQS, R * R)
        score_part = jnp.dot(grads, queries.astype(jnp.float32).T, precision=lax.Precision.HIGHEST)
        return (downstream, (grads, score_part))
    final_grad, outputs = lax.scan(layer_step, out_grad, (section_input, weights, gains, proj_seeds, query_grads), reverse=True)
    projected_grads, score_parts = outputs
    return (projected_grads, lax.optimization_barrier(jnp.sum(score_parts, axis=0)))
```

```python
import functools
import math

import jax
import jax.numpy as jnp
from jax import lax
from jax.experimental import pallas as pl
from jax.experimental.pallas import tpu as pltpu
from jax.sharding import PartitionSpec as P

R = 64
SEQS = 2
eps = 1e-05
F32 = jnp.float32
BF16 = jnp.bfloat16
MESH = pl.DeviceIdType.MESH
NT = (((1,), (1,)), ((), ()))
LAG = 3
GAP = 2
LATE = 0


def sign_rows(seed_value, row_start, row_count, scale):
    row_index = lax.broadcasted_iota(jnp.int32, (R, row_count), 1) + row_start
    col_index = lax.broadcasted_iota(jnp.int32, (R, row_count), 0)
    mixing = row_index * 40503 + col_index * 9973 + (seed_value * 7919 + 12345)
    mixing = mixing ^ (mixing >> 13)
    mixing = mixing * 1274126177
    mixing = mixing ^ (mixing >> 16)
    parity = (mixing >> 10) & 1
    return jnp.where(parity == 1, scale, -scale).astype(BF16)


def kernel(
    sections, nd, nz,
    x_hbm, w_hbm, gain_ref, seed_ref, og_ref, q_ref,
    out_ref,
    a_buf, inf_buf, ps_buf, pr_buf, slope_buf, ui_buf, uii_buf, gp_buf,
    gns_buf, gnr_buf, dot_buf, up_buf, g_buf, gr_buf, sc_buf,
    x_ref, w_ref, sum_buf, norm_buf, rad_buf, turn_buf, mean_buf, left_buf, pick_buf,
    a_ss, a_rs, inf_ss, inf_rs, p_ss, p_rs, og_ss, og_rs, gp_ss, gp_rs,
    gn_ss, gn_rs, dt_ss, dt_rs, up_ss, up_rs, uii_ss, uii_rs,
    g_ss, g_rs, sc_ss, sc_rs, in_sem, go_sem, far_sem,
):
    s = lax.axis_index("section")
    d = lax.axis_index("dp")
    z = lax.axis_index("tensor")
    tok, width = x_hbm.shape
    feat = width // nz
    cols = width // nd
    sub = tok // nz
    at_top = s == sections - 1
    below_top = s == sections - 2
    lower = s > 0
    z_start = pl.multiple_of(z * feat, feat)
    d_start = pl.multiple_of(d * cols, cols)
    sub_start = pl.multiple_of(z * sub, sub)
    sub_start_d = pl.multiple_of(d * sub, sub)

    def dev(s_to, d_to, z_to):
        return {"section": s_to, "dp": d_to, "tensor": z_to}

    def remote(src, dst, ss, rs, to):
        return pltpu.make_async_remote_copy(
            src_ref=src, dst_ref=dst, send_sem=ss, recv_sem=rs, device_id=to, device_id_type=MESH
        )

    x_load = pltpu.make_async_copy(x_hbm, x_ref, in_sem.at[0])
    w_load = pltpu.make_async_copy(w_hbm, w_ref, in_sem.at[1])
    x_load.start()
    w_load.start()

    barrier = pltpu.get_barrier_semaphore()
    column = sections * nz
    here = s * nz + z

    def signal_column(sem):
        for o in range(1, column):
            to = lax.rem(here + o, column)
            pl.semaphore_signal(
                sem, inc=1, device_id=dev(to // nz, d, lax.rem(to, nz)), device_id_type=MESH
            )

    for o in range(1, nd):
        pl.semaphore_signal(
            barrier, inc=1, device_id=dev(s, lax.rem(d + o, nd), z), device_id_type=MESH
        )
    signal_column(barrier)

    x_load.wait()
    hidden = x_ref[...].astype(F32)
    radius = jnp.sqrt(jnp.mean(hidden * hidden, axis=1, keepdims=True) + eps)
    gain_z = gain_ref[:, pl.ds(z_start, feat)]
    normed_z = x_ref[:, pl.ds(z_start, feat)].astype(F32) / radius
    norm_buf[...] = normed_z
    rad_buf[...] = jnp.broadcast_to(radius, rad_buf.shape)
    a_buf[d] = (normed_z * gain_z).astype(BF16)

    pl.semaphore_wait(barrier, nd - 1 + column - 1)

    def a_copy(o):
        to = lax.rem(d + o, nd)
        return remote(a_buf.at[d], a_buf.at[d], a_ss.at[o], a_rs.at[o], dev(s, to, z))

    @pl.when(jnp.logical_not(below_top))
    def _():
        for o in range(1, nd):
            a_copy(o).start()

    def og_copy(o):
        to = lax.rem(d + o, nd)
        src = og_ref.at[pl.ds(sub_start, sub), pl.ds(pl.multiple_of(to * cols, cols), cols)]
        return remote(src, ui_buf.at[d], og_ss.at[o], og_rs.at[o], dev(s, to, z))

    def ui_load():
        src = og_ref.at[pl.ds(sub_start, sub), pl.ds(d_start, cols)]
        return pltpu.make_async_copy(src, ui_buf.at[d], in_sem.at[2])

    def uii_load():
        return pltpu.make_async_copy(og_ref.at[:, pl.ds(z_start, feat)], uii_buf, in_sem.at[3])

    @pl.when(at_top)
    def _():
        for o in range(1, nd):
            og_copy(o).start()
        ui_load().start()
        uii_load().start()

    @pl.when(below_top)
    def _():
        pl.semaphore_wait(go_sem.at[0], 1)
        for o in range(1, nd):
            a_copy(o).start()

    signal_column(far_sem.at[0])

    w_load.wait()

    def p_copy(o, block):
        to = lax.rem(z + o, nz)
        return remote(
            ps_buf.at[to, block], pr_buf.at[z, block], p_ss.at[o, block], p_rs.at[o, block],
            dev(s, d, to),
        )

    for o in range(nd):
        block = lax.rem(d + nd - o, nd)
        if o:
            a_copy(o).wait_recv()
        part = jnp.dot(a_buf[block], w_ref[...], preferred_element_type=F32).astype(BF16)
        for zt in range(nz):
            ps_buf[zt, block] = part[zt * sub : (zt + 1) * sub, :]

        @pl.when(jnp.logical_not(below_top))
        def _():
            for oz in range(1, nz):
                p_copy(oz, block).start()

    for o in range(1, nd):
        a_copy(o).wait_send()

    def go(which):
        pl.semaphore_signal(
            go_sem.at[which], inc=1, device_id=dev(jnp.maximum(s - 1, 0), d, z), device_id_type=MESH
        )

    if sections > 1:
        @pl.when(at_top)
        def _():
            go(0)

    scale = 1.0 / math.sqrt(width)
    x_sub = x_ref[pl.ds(sub_start, sub), :].astype(F32)
    radius_sub = jnp.sqrt(jnp.mean(x_sub * x_sub, axis=1, keepdims=True) + eps)
    lifted_sub = (x_sub / radius_sub * gain_ref[...]).astype(BF16)
    table_in = sign_rows(seed_ref[0, 0], 0, width, scale)
    inf_buf[d] = lax.dot_general(lifted_sub, table_in, NT, preferred_element_type=F32)

    def inf_copy(o):
        to = lax.rem(d + o, nd)
        return remote(inf_buf.at[d], inf_buf.at[d], inf_ss.at[o], inf_rs.at[o], dev(s, to, z))

    for o in range(1, nd):
        inf_copy(o).start()


    piece = R * R // nz
    per_seq = nd * sub // SEQS

    def spread():
        for o in range(1, nd):
            inf_copy(o).wait_recv()
        in_feat = inf_buf[...].reshape(nd * sub, R).astype(BF16)
        for zt in range(nz):
            entry = lax.broadcasted_iota(jnp.int32, (R, piece), 1) + zt * piece
            which = lax.broadcasted_iota(jnp.int32, (R, piece), 0)
            pick_in = (entry // R == which).astype(F32).astype(BF16)
            pick_buf[zt] = (entry % R == which).astype(F32).astype(BF16)
            left_buf[zt] = jnp.dot(in_feat, pick_in, preferred_element_type=F32)

    @pl.when(jnp.logical_not(at_top))
    def _():
        spread()

    if sections > 1:
        @pl.when(below_top)
        def _():
            pl.semaphore_wait(go_sem.at[1], 1)
            for o in range(nd):
                block = lax.rem(d + nd - o, nd)
                for oz in range(1, nz):
                    p_copy(oz, block).start()

    table_out = sign_rows(seed_ref[0, 1], d_start, cols, scale)

    def gp_copy(o, block):
        to = lax.rem(z + o, nz)
        return remote(
            gp_buf.at[z, block], gp_buf.at[z, block], gp_ss.at[o, block], gp_rs.at[o, block],
            dev(s, d, to),
        )

    for o in range(nd):
        block = lax.rem(d + nd - o, nd)
        summed = ps_buf[z, block].astype(F32)
        for oz in range(1, nz):
            p_copy(oz, block).wait_recv()
            summed = summed + pr_buf[lax.rem(z + nz - oz, nz), block].astype(F32)
        sig = jax.nn.sigmoid(summed)
        slope = sig * (1.0 + summed * (1.0 - sig))
        sum_buf[block] = summed
        slope_buf[block] = slope

        @pl.when(at_top)
        def _():
            if o:
                og_copy(o).wait_recv()
            else:
                ui_load().wait()
            gp_buf[z, block] = (ui_buf[block].astype(F32) * slope).astype(BF16)
            if sections > 1:
                for oz in range(1, nz):
                    gp_copy(oz, block).start()

    def up_copy(zt, source):
        return remote(
            up_buf.at[pl.ds(zt * sub, sub)], ui_buf.at[source], up_ss.at[zt], up_rs.at[source],
            dev(jnp.maximum(s - 1, 0), z, zt),
        )

    def uii_copy():
        return remote(up_buf, uii_buf, uii_ss.at[0], uii_rs.at[0], dev(jnp.maximum(s - 1, 0), d, z))

    @pl.when(at_top)
    def _():
        uii_load().wait()
        spread()

    @pl.when(jnp.logical_not(at_top))
    def _():
        for source in range(nd):
            up_copy(0, source).wait_recv()
        gp_buf[z] = (ui_buf[...].astype(F32) * slope_buf[...]).astype(BF16)

        @pl.when(lower)
        def _():
            for block in range(nd):
                for oz in range(1, nz):
                    gp_copy(oz, block).start()

    pl.semaphore_wait(far_sem.at[0], column - 1)
    grad_pre = gp_buf[z]
    plane = nd * nz
    mine = d * nz + z

    def dt_copy(o):
        to = lax.rem(mine + o, plane)
        return remote(
            dot_buf.at[mine], dot_buf.at[mine], dt_ss.at[o], dt_rs.at[o],
            dev(s, to // nz, lax.rem(to, nz)),
        )

    @pl.when(lower)
    def _():
        pre = gp_buf[z].astype(F32) * sum_buf[...]
        own_dot = jnp.sum(pre.reshape(nd * sub, cols), axis=1, keepdims=True)
        dot_buf[mine] = jnp.broadcast_to(own_dot, (tok, tok)).T[:8, :]
        for o in range(1, plane):
            dt_copy(o).start()

    out_feat = lax.dot_general(
        grad_pre.reshape(nd * sub, cols), table_out, NT, preferred_element_type=F32
    ).astype(BF16)
    for zt in range(nz):
        product = left_buf[zt] * jnp.dot(out_feat, pick_buf[zt], preferred_element_type=F32)
        for k in range(SEQS):
            g_buf[zt, k : k + 1, :] = jnp.sum(
                product[k * per_seq : (k + 1) * per_seq], axis=0, keepdims=True
            )

    def g_copy(o):
        to = lax.rem(mine + o, plane)
        return remote(
            g_buf.at[lax.rem(to, nz)], gr_buf.at[mine], g_ss.at[o], g_rs.at[o],
            dev(s, to // nz, lax.rem(to, nz)),
        )

    for o in range(1, plane):
        g_copy(o).start()
    gr_buf[mine] = g_buf[z]

    def gn_copy(o):
        to = lax.rem(d + nd - o, nd)
        return remote(gns_buf.at[to], gnr_buf.at[d], gn_ss.at[o], gn_rs.at[o], dev(s, to, z))

    @pl.when(lower)
    def _():
        for o in range(nd):
            block = lax.rem(d + nd - o, nd)
            for oz in range(1, nz):
                gp_copy(oz, block).wait_recv()
            if o == nd - 1:
                for each in range(nd):
                    for oz in range(1, nz):
                        gp_copy(oz, each).wait_send()

                @pl.when(at_top)
                def _():
                    go(1)

            rows = gp_buf[:, block].reshape(tok, cols)
            part = lax.dot_general(rows, w_ref[...], NT, preferred_element_type=F32).astype(BF16)
            if o:
                gns_buf[block] = part
                gn_copy(o).start()
            else:
                gnr_buf[d] = part
        for o in range(1, plane):
            dt_copy(o).wait_recv()
        for zt in range(nz):
            dots = dot_buf[zt]
            for dt in range(1, nd):
                dots = dots + dot_buf[dt * nz + zt]
            turn_buf[...] = jnp.broadcast_to(dots[:1, :] * (1.0 / width), (tok, tok)).T
            mean_buf[zt] = turn_buf[pl.ds(sub_start_d, sub), :]
        for o in range(1, nd):
            gn_copy(o).wait_recv()
        if sections > 2:
            @pl.when(jnp.logical_not(at_top))
            def _():
                uii_copy().wait_recv()
        for zt in range(nz):
            rows = pl.ds(zt * sub, sub)
            grad_norm = gnr_buf[0, rows].astype(F32)
            for dt in range(1, nd):
                grad_norm = grad_norm + gnr_buf[dt, rows].astype(F32)
            scaled = grad_norm.astype(BF16).astype(F32) * gain_ref[:, pl.ds(z_start, feat)]
            change = (scaled - norm_buf[rows] * mean_buf[zt][:, :1]) / rad_buf[rows, :1]
            up_buf[rows] = (uii_buf[rows].astype(F32) + change).astype(BF16)
            up_copy(zt, d).start()
        if sections > 2:
            @pl.when(s > 1)
            def _():
                uii_copy().start()

    for o in range(1, plane):
        g_copy(o).wait_recv()
    grads = gr_buf[0]
    for other in range(1, plane):
        grads = grads + gr_buf[other]
    out_ref[:, :piece] = grads
    queries = q_ref[...]
    high = grads.astype(BF16)
    rest = grads - high.astype(F32)
    middle = rest.astype(BF16)
    low = (rest - middle.astype(F32)).astype(BF16)
    part = lax.dot_general(high, queries, NT, preferred_element_type=F32)
    part = part + lax.dot_general(middle, queries, NT, preferred_element_type=F32)
    part = part + lax.dot_general(low, queries, NT, preferred_element_type=F32)
    sc_buf[here] = part

    def sc_copy(o):
        to = lax.rem(here + o, column)
        return remote(
            sc_buf.at[here], sc_buf.at[here], sc_ss.at[o], sc_rs.at[o],
            dev(to // nz, d, lax.rem(to, nz)),
        )

    for o in range(1, column):
        sc_copy(o).start()

    for o in range(1, nd):
        inf_copy(o).wait_send()
    for block in range(nd):
        for oz in range(1, nz):
            p_copy(oz, block).wait_send()

    @pl.when(at_top)
    def _():
        for o in range(1, nd):
            og_copy(o).wait_send()

    @pl.when(lower)
    def _():
        for o in range(1, plane):
            dt_copy(o).wait_send()
        for o in range(1, nd):
            gn_copy(o).wait_send()
        for zt in range(nz):
            up_copy(zt, d).wait_send()
        if sections > 2:
            @pl.when(s > 1)
            def _():
                uii_copy().wait_send()

    for o in range(1, plane):
        g_copy(o).wait_send()
    for o in range(1, column):
        sc_copy(o).wait_recv()
    scores = sc_buf[0]
    for other in range(1, column):
        scores = scores + sc_buf[other]
    out_ref[:, piece : piece + scores.shape[1]] = scores
    for o in range(1, column):
        sc_copy(o).wait_send()


def pair_kernel(
    nd, nz, lag, gap, late,
    x_hbm, w_hbm, gain_ref, seed_ref, og_ref, q_ref,
    out_ref,
    x_ref, w_ref, wide_ref, tab_in, tab_out, norm_buf, rad_buf,
    a_buf, p_buf, un_buf, uo_buf, dn_buf, do_buf,
    og_buf, uii_buf, gp_buf, dot_buf, gns_buf, gnr_buf, xs_buf, xr_buf,
    so_buf, slope_buf, tabr_buf, infs_buf, infr_buf, low_buf,
    left_buf, g_buf, gr_buf, g1_buf, gr1_buf, sc_buf,
    in_sem, go_sem, far_sem,
    a_ss, a_rs, og_ss, og_rs, up_ss, up_rs, dn_ss, dn_rs, gn_ss, gn_rs, xs_ss, xs_rs,
    so_ss, so_rs, side_ss, side_rs, g_ss, g_rs, g1_ss, g1_rs, sc_ss, sc_rs,
):
    s = lax.axis_index("section")
    d = lax.axis_index("dp")
    z = lax.axis_index("tensor")
    tok, width = x_hbm.shape
    feat = width // nz
    cols = width // nd
    sub = tok // nz
    plane = nd * nz
    column = 2 * nz
    piece = R * R // nz
    lanes = tab_out.shape[0]
    half = tok // 2
    per_seq = nd // SEQS
    at_top = s == 1
    z_start = pl.multiple_of(z * feat, feat)
    d_start = pl.multiple_of(d * cols, cols)
    here = s * nz + z
    mine = d * nz + z
    scale = 1.0 / math.sqrt(width)

    def dev(s_to, d_to, z_to):
        return {"section": s_to, "dp": d_to, "tensor": z_to}

    def flip(j):
        to, bit = d, 1
        while bit < nd:
            flag = (j // bit) % 2 if isinstance(j, int) else lax.rem(lax.div(j, bit), 2)
            to = to + flag * bit * (1 - 2 * lax.rem(lax.div(d, bit), 2))
            bit *= 2
        return to

    def remote(src, dst, ss, rs, to):
        return pltpu.make_async_remote_copy(
            src_ref=src, dst_ref=dst, send_sem=ss, recv_sem=rs, device_id=to, device_id_type=MESH
        )

    def signal(sem, to):
        pl.semaphore_signal(sem, inc=1, device_id=to, device_id_type=MESH)

    x_load = pltpu.make_async_copy(x_hbm, x_ref, in_sem.at[0])
    w_load = pltpu.make_async_copy(w_hbm, w_ref, in_sem.at[1])
    x_load.start()
    w_load.start()
    barrier = pltpu.get_barrier_semaphore()

    def signal_column(sem):
        for o in range(1, column):
            to = lax.rem(here + o, column)
            signal(sem, dev(to // nz, d, lax.rem(to, nz)))

    for j in range(1, nd):
        signal(barrier, dev(s, flip(j), z))
    signal_column(barrier)

    ui_load = pltpu.make_async_copy(og_ref.at[:, pl.ds(d_start, cols)], og_buf.at[0], in_sem.at[2])
    uii_load = pltpu.make_async_copy(og_ref.at[:, pl.ds(z_start, feat)], uii_buf, in_sem.at[3])

    @pl.when(at_top)
    def _():
        ui_load.start()
        uii_load.start()

    table_row = jnp.where(at_top, d_start, z_start)
    tab_out[:R] = sign_rows(seed_ref[0, 1], table_row, cols, scale)
    tab_out[R:] = jnp.zeros((lanes - R, cols), BF16)
    tab_in[...] = sign_rows(seed_ref[0, 0], 0, width, scale)

    x_load.wait()
    hidden = x_ref[...].astype(F32)
    radius = jnp.sqrt(jnp.mean(hidden * hidden, axis=1, keepdims=True) + eps)
    normed_z = x_ref[:, pl.ds(z_start, feat)].astype(F32) / radius
    norm_buf[...] = normed_z
    rad_buf[...] = jnp.broadcast_to(radius, rad_buf.shape)
    a_buf[0] = (normed_z * gain_ref[:, pl.ds(z_start, feat)]).astype(BF16)

    pl.semaphore_wait(barrier, nd - 1 + column - 1)

    def a_copy(j, h, via=0):
        rows = pl.ds(h * half, half)
        return remote(
            a_buf.at[via, rows], a_buf.at[j, rows], a_ss.at[j, h], a_rs.at[j, h], dev(s, flip(j - via), z)
        )

    def a_start():
        a_copy(1, 0).start()
        a_copy(2, 1).start()
        a_copy(1, 1).start()
        a_copy(2, 0).start()

    def a_wait(j):
        if j == 1:
            a_copy(1, 0).wait_recv()
            a_copy(3, 0, 1).start()
            a_copy(2, 1).wait_recv()
            a_copy(3, 1, 2).start()
            a_copy(1, 1).wait_recv()
        if j == 2:
            a_copy(2, 0).wait_recv()
        if j == 3:
            for h in range(2):
                a_copy(3, h).wait_recv()

    def a_sent():
        for j in range(1, nd):
            for h in range(2):
                a_copy(j, h).wait_send()

    def og_copy(j):
        to = flip(j)
        src = og_ref.at[:, pl.ds(pl.multiple_of(to * cols, cols), cols)]
        return remote(src, og_buf.at[j], og_ss.at[j], og_rs.at[j], dev(s, to, z))

    @pl.when(at_top)
    def _():
        a_start()
        og_copy(1).start()
        og_copy(2).start()

    signal_column(far_sem.at[0])
    w_load.wait()

    def in_features():
        lifted = (x_ref[...].astype(F32) / rad_buf[:, :1] * gain_ref[...]).astype(BF16)
        return lax.dot_general(lifted, tab_in[...], NT, preferred_element_type=F32).astype(BF16)

    def pick_in(zt):
        entry = lax.broadcasted_iota(jnp.int32, (R, piece), 1) + zt * piece
        which = lax.broadcasted_iota(jnp.int32, (R, piece), 0)
        return (entry // R == which).astype(F32).astype(BF16)

    def pick_out():
        entry = lax.broadcasted_iota(jnp.int32, (R, piece), 1)
        which = lax.broadcasted_iota(jnp.int32, (R, piece), 0)
        return (entry % R == which).astype(F32).astype(BF16)

    def up_copy(c, first):
        src = p_buf.at[c] if first else uo_buf.at[c]
        return remote(src, un_buf.at[c], up_ss.at[c], up_rs.at[c], dev(s, d, jnp.minimum(z + 1, nz - 1)))

    def dn_copy(c, first):
        src = p_buf.at[c] if first else do_buf.at[c]
        return remote(src, dn_buf.at[c], dn_ss.at[c], dn_rs.at[c], dev(s, d, jnp.maximum(z - 1, 0)))

    def gn_copy(j, row, rows, h, to):
        return remote(
            gns_buf.at[j, pl.ds(row, rows)], gnr_buf.at[j, pl.ds(row, rows)],
            gn_ss.at[j, h], gn_rs.at[j, h], dev(s, to, z),
        )

    def xs_copy(j, row, rows, h, to):
        return remote(
            xs_buf.at[j, pl.ds(row, rows)], xr_buf.at[j, pl.ds(row, rows)],
            xs_ss.at[j, h], xs_rs.at[j, h], dev(s, to, z),
        )

    def so_copy(j, to):
        return remote(so_buf.at[j], slope_buf.at[z], so_ss.at[j], so_rs.at[z], dev(1, to, d))

    def so_arrival(k):
        return remote(so_buf.at[0], slope_buf.at[k], so_ss.at[0], so_rs.at[k], dev(0, d, z))

    def back(j, row, rows):
        pre = gp_buf[j, pl.ds(row, rows)]
        both = jnp.dot(pre, wide_ref[...], preferred_element_type=F32)
        dot = dot_buf[j, pl.ds(row, rows)]
        high = dot.astype(BF16).astype(F32)
        lane = lax.broadcasted_iota(jnp.int32, (rows, lanes), 1)
        extra = jnp.where(lane == R, high, jnp.where(lane == R + 1, dot - high, both[:, feat:]))
        return both[:, :feat].astype(BF16), extra.astype(BF16)

    def slope_of(total):
        sig = jax.nn.sigmoid(total)
        return sig * (1.0 + total * (1.0 - sig))

    lag_up = z * lag
    lag_dn = (nz - 1 - z) * lag
    lag_all = jnp.maximum(lag_up, lag_dn) + late
    slots = plane + gap + (nz - 1) * lag + late

    def chunk_at(v):
        valid = jnp.logical_and(v >= 0, v < plane + gap)
        valid = jnp.logical_and(valid, jnp.logical_or(v < nz, v >= nz + gap))
        return jnp.where(v < nz, v, v - gap), valid

    def relay(c, valid, gets, sends, copy, inbox, outbox):

        @pl.when(jnp.logical_and(valid, gets))
        def _():
            copy(c, True).wait_recv()

        @pl.when(jnp.logical_and(valid, jnp.logical_and(sends, jnp.logical_not(gets))))
        def _():
            copy(c, True).start()

        @pl.when(jnp.logical_and(valid, jnp.logical_and(sends, gets)))
        def _():
            outbox[c] = (inbox[c].astype(F32) + p_buf[c].astype(F32)).astype(BF16)
            copy(c, False).start()

    def sweep(on_block, on_total):
        def slot(i, carry):
            for j in range(nd):
                @pl.when(i == (j * nz + gap if j else 0))
                def _(j=j):
                    on_block(j)
                    multiply(j)

            c, valid = chunk_at(i - lag_up)
            relay(c, valid, z > 0, z < nz - 1, up_copy, un_buf, uo_buf)
            c, valid = chunk_at(i - lag_dn)
            relay(c, valid, z < nz - 1, z > 0, dn_copy, dn_buf, do_buf)
            c, valid = chunk_at(i - lag_all)
            q = lax.rem(jnp.maximum(c, 0), nz)
            j_now = lax.div(jnp.maximum(c, 0), nz)

            def total_of(up, dn):
                total = p_buf[c].astype(F32)
                if up:
                    total = total + un_buf[c].astype(F32)
                if dn:
                    total = total + dn_buf[c].astype(F32)
                on_total(j_now, q, total)

            @pl.when(jnp.logical_and(valid, z == 0))
            def _():
                total_of(False, True)

            @pl.when(jnp.logical_and(valid, z == nz - 1))
            def _():
                total_of(True, False)

            @pl.when(jnp.logical_and(valid, jnp.logical_and(z > 0, z < nz - 1)))
            def _():
                total_of(True, True)

            @pl.when(valid)
            def _():
                after_total(j_now, q)

            return carry

        lax.fori_loop(0, slots, slot, 0)

    def multiply(j):
        part = jnp.dot(a_buf[j], w_ref[...], preferred_element_type=F32).astype(BF16)
        for q in range(nz):
            p_buf[j * nz + q] = part[q * sub : (q + 1) * sub]

    def after_total(j, q):
        @pl.when(jnp.logical_and(q == nz - 1, j == 0))
        def _():
            gnr_buf[0], xr_buf[0] = back(0, 0, tok)

        @pl.when(jnp.logical_and(q == nz - 1, jnp.logical_and(j > 0, j < nd - 1)))
        def _():
            gns_buf[j], xs_buf[j] = back(j, 0, tok)
            gn_copy(j, 0, tok, 0, flip(j)).start()
            xs_copy(j, 0, tok, 0, flip(j)).start()

        for h in range(2):
            @pl.when(jnp.logical_and(q == (h + 1) * nz // 2 - 1, j == nd - 1))
            def _(h=h):
                last, rows = nd - 1, pl.ds(h * half, half)
                gns_buf[last, rows], xs_buf[last, rows] = back(last, h * half, half)
                gn_copy(last, h * half, half, h, flip(last)).start()
                xs_copy(last, h * half, half, h, flip(last)).start()

    def sweep_sent():
        def one(c, carry):
            @pl.when(z < nz - 1)
            def _():
                up_copy(c, True).wait_send()

            @pl.when(z > 0)
            def _():
                dn_copy(c, True).wait_send()

            return carry

        lax.fori_loop(0, plane, one, 0)

    def g_copy(o):
        return remote(g_buf.at[o % nz], gr_buf.at[mine], g_ss.at[o], g_rs.at[mine], dev(0, o // nz, o % nz))

    def g_arrival(o):
        return remote(g_buf.at[0], gr_buf.at[o], g_ss.at[o], g_rs.at[o], dev(1, d, z))

    def g1_copy(j):
        return remote(g1_buf, gr1_buf.at[j], g1_ss.at[j], g1_rs.at[j], dev(1, flip(j), z))

    def side_copy(which):
        src, dst = ((infs_buf, infr_buf), (tab_out, tabr_buf))[which]
        return remote(src, dst, side_ss.at[which], side_rs.at[which], dev(1, d, z))

    def side_arrival(which):
        src, dst = ((infs_buf, infr_buf), (tab_out, tabr_buf))[which]
        return remote(src, dst, side_ss.at[which], side_rs.at[which], dev(0, d, z))

    def sc_copy(o):
        to = lax.rem(here + o, column)
        return remote(
            sc_buf.at[here], sc_buf.at[here], sc_ss.at[o], sc_rs.at[o], dev(to // nz, d, lax.rem(to, nz))
        )

    def score():
        grads = out_ref[:, :piece]
        queries = q_ref[...]
        high = grads.astype(BF16)
        rest = grads - high.astype(F32)
        middle = rest.astype(BF16)
        low = (rest - middle.astype(F32)).astype(BF16)
        part = lax.dot_general(high, queries, NT, preferred_element_type=F32)
        part = part + lax.dot_general(middle, queries, NT, preferred_element_type=F32)
        part = part + lax.dot_general(low, queries, NT, preferred_element_type=F32)
        sc_buf[here] = part
        for o in range(1, column):
            sc_copy(o).start()

    @pl.when(at_top)
    def _():
        def on_block(j):
            if j == 1:
                wide_ref[:, :feat] = w_ref[...].T
                wide_ref[:, feat:] = tab_out[...].T
            a_wait(j)
            if j == 1:
                signal(go_sem.at[0], dev(0, d, z))
            if j == 2:
                og_copy(3).start()

        def on_total(j, q, total):
            for each in range(nd):
                @pl.when(jnp.logical_and(q == 0, j == each))
                def _(each=each):
                    if each:
                        og_copy(each).wait_recv()
                    else:
                        ui_load.wait()

            rows = pl.ds(pl.multiple_of(q * sub, sub), sub)
            pre = (og_buf[j, rows].astype(F32) * slope_of(total)).astype(BF16)
            gp_buf[j, rows] = pre
            dot = jnp.sum(pre.astype(F32) * total, axis=1, keepdims=True)
            dot_buf[j, rows] = jnp.broadcast_to(dot, (sub, lanes))

        sweep(on_block, on_total)

        in_feat = in_features()
        g_left = jnp.dot(in_feat, pick_in(z), preferred_element_type=F32)
        left_buf[nz] = g_left
        for which in range(2):
            side_arrival(which).wait_recv()
        for zt in range(nz):
            left_buf[zt] = jnp.dot(infr_buf[:, :R], pick_in(zt), preferred_element_type=F32)
        uii_load.wait()
        pl.semaphore_wait(far_sem.at[0], column - 1)
        for k in range(nz):
            so_arrival(k).wait_recv()
        for j in range(1, nd - 1):
            gn_copy(j, 0, tok, 0, d).wait_recv()
            xs_copy(j, 0, tok, 0, d).wait_recv()
        for k in range(nz):
            if k * 2 % nz == 0:
                h = k * 2 // nz
                gn_copy(nd - 1, h * half, half, h, d).wait_recv()
                xs_copy(nd - 1, h * half, half, h, d).wait_recv()
            rows = pl.ds(k * sub, sub)
            grad_norm = gnr_buf[0, rows].astype(F32)
            extra = xr_buf[0, rows].astype(F32)
            for j in range(1, nd):
                grad_norm = grad_norm + gnr_buf[j, rows].astype(F32)
                extra = extra + xr_buf[j, rows].astype(F32)
            dot_buf[0, rows] = extra
            mean_dot = (extra[:, R : R + 1] + extra[:, R + 1 : R + 2]) * (1.0 / width)
            scaled = grad_norm.astype(BF16).astype(F32) * gain_ref[:, pl.ds(z_start, feat)]
            change = (scaled - norm_buf[rows] * mean_dot) / rad_buf[rows, :1]
            upstream = (uii_buf[rows].astype(F32) + change).astype(BF16)
            low_buf[rows] = (upstream.astype(F32) * slope_buf[k].astype(F32)).astype(BF16)
        out_low = lax.dot_general(low_buf[...], tabr_buf[...], NT, preferred_element_type=F32)
        spread = pick_out()
        right = jnp.dot(out_low[:, :R].astype(BF16), spread, preferred_element_type=F32)
        for zt in range(nz):
            g_buf[zt] = jnp.sum(left_buf[zt] * right, axis=0, keepdims=True)
        for o in range(plane):
            g_copy(o).start()

        right = jnp.dot(dot_buf[0, :, :R].astype(BF16), spread, preferred_element_type=F32)
        own = jnp.sum(left_buf[nz] * right, axis=0, keepdims=True)
        g1_buf[...] = own
        for j in range(1, nd):
            g1_copy(j).start()
        gr1_buf[0] = own
        for j in range(1, nd):
            g1_copy(j).wait_recv()
        for k in range(SEQS):
            row = jnp.zeros((1, piece), F32)
            for group in range(SEQS):
                held = gr1_buf[group * per_seq]
                for j in range(group * per_seq + 1, (group + 1) * per_seq):
                    held = held + gr1_buf[j]
                row = row + jnp.where(lax.div(flip(group * per_seq), per_seq) == k, held, 0.0)
            out_ref[k : k + 1, :piece] = row
        score()
        for j in range(1, nd):
            og_copy(j).wait_send()
            g1_copy(j).wait_send()
        for j in range(1, nd - 1):
            gn_copy(j, 0, tok, 0, d).wait_send()
            xs_copy(j, 0, tok, 0, d).wait_send()
        for h in range(2):
            gn_copy(nd - 1, h * half, half, h, d).wait_send()
            xs_copy(nd - 1, h * half, half, h, d).wait_send()
        for o in range(plane):
            g_copy(o).wait_send()
        a_sent()
        sweep_sent()

    @pl.when(jnp.logical_not(at_top))
    def _():
        def chain_up(block, valid):
            for q in reversed(range(nz)):
                relay(
                    block * nz + q, valid, jnp.logical_and(z > 0, q >= z), q > z, up_copy, un_buf, uo_buf
                )

        def chain_dn(block, valid):
            for q in range(nz):
                relay(
                    block * nz + q, valid, jnp.logical_and(z < nz - 1, q <= z), q < z, dn_copy, dn_buf, do_buf
                )

        def lower_slope(block):
            c = block * nz + z
            total = p_buf[c].astype(F32)
            total = total + jnp.where(z > 0, un_buf[c].astype(F32), 0.0)
            total = total + jnp.where(z < nz - 1, dn_buf[c].astype(F32), 0.0)
            so_buf[block] = slope_of(total).astype(BF16)
            so_copy(block, flip(block)).start()

        far_end = jnp.maximum(z, nz - 1 - z)
        multiply(0)
        chain_up(0, z == 0)
        chain_dn(0, z == nz - 1)
        infs_buf[:, :R] = in_features()
        infs_buf[:, R:] = jnp.zeros((tok, lanes - R), BF16)
        for which in range(2):
            side_copy(which).start()
        pl.semaphore_wait(go_sem.at[0], 1)
        a_start()
        pl.semaphore_wait(far_sem.at[0], column - 1)
        for hop in range(1, nz):
            chain_up(0, z == hop)
            chain_dn(0, nz - 1 - z == hop)
        lower_slope(0)
        for block in range(1, nd):
            a_wait(block)
            multiply(block)
            chain_up(block, z == 0)
            chain_dn(block, z == nz - 1)
        for step in range(1, nd + nz - 2):
            block = step + 1 - z
            chain_up(block, jnp.logical_and(z > 0, jnp.logical_and(block >= 1, block < nd)))
            block = step + 2 - nz + z
            chain_dn(block, jnp.logical_and(z < nz - 1, jnp.logical_and(block >= 1, block < nd)))
            block = step + 1 - far_end

            @pl.when(jnp.logical_and(block >= 1, block < nd))
            def _(block=block):
                lower_slope(block)

        for o in range(plane):
            g_arrival(o).wait_recv()
        for k in range(SEQS):
            held = gr_buf[k * per_seq * nz]
            for o in range(k * per_seq * nz + 1, (k + 1) * per_seq * nz):
                held = held + gr_buf[o]
            out_ref[k : k + 1, :piece] = held
        score()
        a_sent()
        for j in range(nd):
            so_copy(j, d).wait_send()
        for which in range(2):
            side_copy(which).wait_send()
        for j in range(nd):
            for q in range(nz):
                @pl.when(q > z)
                def _(c=j * nz + q):
                    up_copy(c, True).wait_send()

                @pl.when(q < z)
                def _(c=j * nz + q):
                    dn_copy(c, True).wait_send()

    for o in range(1, column):
        sc_copy(o).wait_recv()
    scores = sc_buf[0]
    for other in range(1, column):
        scores = scores + sc_buf[other]
    out_ref[:, piece : piece + scores.shape[1]] = scores
    for o in range(1, column):
        sc_copy(o).wait_send()


def pair_call(nd, nz, tok, width, queries):
    feat, cols, sub, plane, column = width // nz, width // nd, tok // nz, nd * nz, 2 * nz
    piece, lanes = R * R // nz, 2 * R
    dma = pltpu.SemaphoreType.DMA
    sems = []
    for shape in (
        (nd, 2), (nd,), (plane,), (plane,), (nd, 2), (nd, 2),
    ):
        sems += [dma(shape), dma(shape)]
    sems += [dma((nd,)), dma((nz,)), dma((2,)), dma((2,)), dma((plane,)), dma((plane,))]
    sems += [dma((nd,)), dma((nd,)), dma((column,)), dma((column,))]
    vmem = pl.BlockSpec(memory_space=pltpu.VMEM)
    hbm = pl.BlockSpec(memory_space=pl.ANY)
    chunks = pltpu.VMEM((plane, sub, cols), BF16)
    blocks = pltpu.VMEM((nd, tok, cols), BF16)
    return pl.pallas_call(
        functools.partial(pair_kernel, nd, nz, LAG, GAP, LATE),
        out_shape=pltpu.VMEM((SEQS, piece + queries), F32),
        in_specs=[hbm, hbm, vmem, pl.BlockSpec(memory_space=pltpu.SMEM), hbm, vmem],
        out_specs=vmem,
        scratch_shapes=[
            pltpu.VMEM((tok, width), BF16),
            pltpu.VMEM((feat, cols), BF16),
            pltpu.VMEM((cols, feat + lanes), BF16),
            pltpu.VMEM((R, width), BF16),
            pltpu.VMEM((lanes, cols), BF16),
            pltpu.VMEM((tok, feat), F32),
            pltpu.VMEM((tok, 128), F32),
            blocks, chunks, chunks, chunks, chunks, chunks,
            blocks,
            pltpu.VMEM((tok, feat), BF16),
            blocks,
            pltpu.VMEM((nd, tok, lanes), F32),
            blocks, blocks,
            pltpu.VMEM((nd, tok, lanes), BF16),
            pltpu.VMEM((nd, tok, lanes), BF16),
            pltpu.VMEM((nd, sub, cols), BF16),
            pltpu.VMEM((nz, sub, cols), BF16),
            pltpu.VMEM((lanes, cols), BF16),
            pltpu.VMEM((tok, lanes), BF16),
            pltpu.VMEM((tok, lanes), BF16),
            pltpu.VMEM((tok, cols), BF16),
            pltpu.VMEM((nz + 1, tok, piece), F32),
            pltpu.VMEM((nz, 1, piece), F32),
            pltpu.VMEM((plane, 1, piece), F32),
            pltpu.VMEM((1, piece), F32),
            pltpu.VMEM((nd, 1, piece), F32),
            pltpu.VMEM((column, SEQS, queries), F32),
            dma((4,)),
            pltpu.SemaphoreType.REGULAR((2,)),
            pltpu.SemaphoreType.REGULAR((1,)),
            *sems,
        ],
        compiler_params=pltpu.CompilerParams(
            collective_id=0, has_side_effects=True, vmem_limit_bytes=60 * 1024 * 1024
        ),
    )


def stack_call(sections, nd, nz, tok, width, queries):
    feat, cols = width // nz, width // nd
    sub = tok // nz
    piece = R * R // nz
    column = sections * nz
    plane = nd * nz
    vmem = pl.BlockSpec(memory_space=pltpu.VMEM)
    hbm = pl.BlockSpec(memory_space=pl.ANY)
    dma = pltpu.SemaphoreType.DMA
    sems = []
    for shape in ((nd,), (nd,), (nz, nd), (nd,), (nz, nd), (nd,), (plane,)):
        sems += [dma(shape), dma(shape)]
    sems += [dma((nz,)), dma((nd,)), dma((1,)), dma((1,))]
    sems += [dma((plane,)), dma((plane,)), dma((column,)), dma((column,))]
    return pl.pallas_call(
        functools.partial(kernel, sections, nd, nz),
        out_shape=jax.ShapeDtypeStruct((SEQS, piece + queries), F32),
        in_specs=[hbm, hbm, vmem, pl.BlockSpec(memory_space=pltpu.SMEM), hbm, vmem],
        out_specs=vmem,
        scratch_shapes=[
            pltpu.VMEM((nd, tok, feat), BF16),
            pltpu.VMEM((nd, sub, R), F32),
            pltpu.VMEM((nz, nd, sub, cols), BF16),
            pltpu.VMEM((nz, nd, sub, cols), BF16),
            pltpu.VMEM((nd, sub, cols), F32),
            pltpu.VMEM((nd, sub, cols), BF16),
            pltpu.VMEM((tok, feat), BF16),
            pltpu.VMEM((nz, nd, sub, cols), BF16),
            pltpu.VMEM((nd, tok, feat), BF16),
            pltpu.VMEM((nd, tok, feat), BF16),
            pltpu.VMEM((plane, 8, tok), F32),
            pltpu.VMEM((tok, feat), BF16),
            pltpu.VMEM((nz, SEQS, piece), F32),
            pltpu.VMEM((plane, SEQS, piece), F32),
            pltpu.VMEM((column, SEQS, queries), F32),
            pltpu.VMEM((tok, width), BF16),
            pltpu.VMEM((feat, cols), BF16),
            pltpu.VMEM((nd, sub, cols), F32),
            pltpu.VMEM((tok, feat), F32),
            pltpu.VMEM((tok, 128), F32),
            pltpu.VMEM((tok, tok), F32),
            pltpu.VMEM((nz, sub, tok), F32),
            pltpu.VMEM((nz, tok, piece), F32),
            pltpu.VMEM((nz, R, piece), BF16),
            *sems,
            dma((4,)),
            pltpu.SemaphoreType.REGULAR((2,)),
            pltpu.SemaphoreType.REGULAR((1,)),
        ],
        compiler_params=pltpu.CompilerParams(
            collective_id=0, has_side_effects=True, vmem_limit_bytes=60 * 1024 * 1024
        ),
    )


def part_outputs(both_ref, grads_ref, scores_ref):
    piece = grads_ref.shape[1]
    grads_ref[...] = both_ref[:, :piece]
    scores_ref[...] = both_ref[:, piece : piece + scores_ref.shape[1]]


def body(section_input, weights, gains, proj_seeds, out_grad, query_grads):
    sections = lax.axis_size("section")
    nd = lax.axis_size("dp")
    nz = lax.axis_size("tensor")
    tok, width = section_input.shape[1:]
    feat = weights.shape[1]
    cols = weights.shape[2]
    assert nd == nz and feat == cols
    piece = R * R // nz
    queries = query_grads.shape[1]
    vmem = pl.BlockSpec(memory_space=pltpu.VMEM)
    paired = sections == 2 and nd == 4 and nz % 2 == 0
    if paired:
        call = pair_call(nd, nz, tok, width, queries)
    else:
        call = stack_call(sections, nd, nz, tok, width, queries)
    out = call(section_input[0], weights[0], gains, proj_seeds, out_grad, query_grads[0])
    if paired:
        out = pltpu.with_memory_space_constraint(out, pltpu.VMEM)
    grads, scores = pl.pallas_call(
        part_outputs,
        out_shape=(
            jax.ShapeDtypeStruct((SEQS, piece), F32),
            jax.ShapeDtypeStruct((SEQS, queries), F32),
        ),
        in_specs=[vmem],
        out_specs=(vmem, vmem),
    )(out)
    return (grads[None], scores)


def solution(mesh):
    in_specs = (
        P("section", "dp", None),
        P("section", "tensor", "dp"),
        P("section", None),
        P("section", None),
        P("dp", None),
        P("section", "dp", "tensor"),
    )
    out_specs = (P("section", None, "tensor"), P(None, "dp"))
    return jax.shard_map(body, mesh=mesh, in_specs=in_specs, out_specs=out_specs, check_vma=False)
```

```python
import functools
import math

import jax
import jax.numpy as jnp
from jax import lax
from jax.experimental import pallas as pl
from jax.experimental.pallas import tpu as pltpu
from jax.sharding import PartitionSpec as P

R = 64
SEQS = 2
eps = 1e-05
F32 = jnp.float32
BF16 = jnp.bfloat16
MESH = pl.DeviceIdType.MESH
NT = (((1,), (1,)), ((), ()))
LAG = 6
GAP = 3
LATE = 0
OGA = 1
OGB = 2


def sign_rows(seed_value, row_start, row_count, scale):
    row_index = lax.broadcasted_iota(jnp.int32, (R, row_count), 1) + row_start
    col_index = lax.broadcasted_iota(jnp.int32, (R, row_count), 0)
    mixing = row_index * 40503 + col_index * 9973 + (seed_value * 7919 + 12345)
    mixing = mixing ^ (mixing >> 13)
    mixing = mixing * 1274126177
    mixing = mixing ^ (mixing >> 16)
    parity = (mixing >> 10) & 1
    return jnp.where(parity == 1, scale, -scale).astype(BF16)


def kernel(
    sections, nd, nz,
    x_hbm, w_hbm, gain_ref, seed_ref, og_ref, q_ref,
    out_ref,
    a_buf, inf_buf, ps_buf, pr_buf, slope_buf, ui_buf, uii_buf, gp_buf,
    gns_buf, gnr_buf, dot_buf, up_buf, g_buf, gr_buf, sc_buf,
    x_ref, w_ref, sum_buf, norm_buf, rad_buf, turn_buf, mean_buf, left_buf, pick_buf,
    a_ss, a_rs, inf_ss, inf_rs, p_ss, p_rs, og_ss, og_rs, gp_ss, gp_rs,
    gn_ss, gn_rs, dt_ss, dt_rs, up_ss, up_rs, uii_ss, uii_rs,
    g_ss, g_rs, sc_ss, sc_rs, in_sem, go_sem, far_sem,
):
    s = lax.axis_index("section")
    d = lax.axis_index("dp")
    z = lax.axis_index("tensor")
    tok, width = x_hbm.shape
    feat = width // nz
    cols = width // nd
    sub = tok // nz
    at_top = s == sections - 1
    below_top = s == sections - 2
    lower = s > 0
    z_start = pl.multiple_of(z * feat, feat)
    d_start = pl.multiple_of(d * cols, cols)
    sub_start = pl.multiple_of(z * sub, sub)
    sub_start_d = pl.multiple_of(d * sub, sub)

    def dev(s_to, d_to, z_to):
        return {"section": s_to, "dp": d_to, "tensor": z_to}

    def remote(src, dst, ss, rs, to):
        return pltpu.make_async_remote_copy(
            src_ref=src, dst_ref=dst, send_sem=ss, recv_sem=rs, device_id=to, device_id_type=MESH
        )

    x_load = pltpu.make_async_copy(x_hbm, x_ref, in_sem.at[0])
    w_load = pltpu.make_async_copy(w_hbm, w_ref, in_sem.at[1])
    x_load.start()
    w_load.start()

    barrier = pltpu.get_barrier_semaphore()
    column = sections * nz
    here = s * nz + z

    def signal_column(sem):
        for o in range(1, column):
            to = lax.rem(here + o, column)
            pl.semaphore_signal(
                sem, inc=1, device_id=dev(to // nz, d, lax.rem(to, nz)), device_id_type=MESH
            )

    for o in range(1, nd):
        pl.semaphore_signal(
            barrier, inc=1, device_id=dev(s, lax.rem(d + o, nd), z), device_id_type=MESH
        )
    signal_column(barrier)

    x_load.wait()
    hidden = x_ref[...].astype(F32)
    radius = jnp.sqrt(jnp.mean(hidden * hidden, axis=1, keepdims=True) + eps)
    gain_z = gain_ref[:, pl.ds(z_start, feat)]
    normed_z = x_ref[:, pl.ds(z_start, feat)].astype(F32) / radius
    norm_buf[...] = normed_z
    rad_buf[...] = jnp.broadcast_to(radius, rad_buf.shape)
    a_buf[d] = (normed_z * gain_z).astype(BF16)

    pl.semaphore_wait(barrier, nd - 1 + column - 1)

    def a_copy(o):
        to = lax.rem(d + o, nd)
        return remote(a_buf.at[d], a_buf.at[d], a_ss.at[o], a_rs.at[o], dev(s, to, z))

    @pl.when(jnp.logical_not(below_top))
    def _():
        for o in range(1, nd):
            a_copy(o).start()

    def og_copy(o):
        to = lax.rem(d + o, nd)
        src = og_ref.at[pl.ds(sub_start, sub), pl.ds(pl.multiple_of(to * cols, cols), cols)]
        return remote(src, ui_buf.at[d], og_ss.at[o], og_rs.at[o], dev(s, to, z))

    def ui_load():
        src = og_ref.at[pl.ds(sub_start, sub), pl.ds(d_start, cols)]
        return pltpu.make_async_copy(src, ui_buf.at[d], in_sem.at[2])

    def uii_load():
        return pltpu.make_async_copy(og_ref.at[:, pl.ds(z_start, feat)], uii_buf, in_sem.at[3])

    @pl.when(at_top)
    def _():
        for o in range(1, nd):
            og_copy(o).start()
        ui_load().start()
        uii_load().start()

    @pl.when(below_top)
    def _():
        pl.semaphore_wait(go_sem.at[0], 1)
        for o in range(1, nd):
            a_copy(o).start()

    signal_column(far_sem.at[0])

    w_load.wait()

    def p_copy(o, block):
        to = lax.rem(z + o, nz)
        return remote(
            ps_buf.at[to, block], pr_buf.at[z, block], p_ss.at[o, block], p_rs.at[o, block],
            dev(s, d, to),
        )

    for o in range(nd):
        block = lax.rem(d + nd - o, nd)
        if o:
            a_copy(o).wait_recv()
        part = jnp.dot(a_buf[block], w_ref[...], preferred_element_type=F32).astype(BF16)
        for zt in range(nz):
            ps_buf[zt, block] = part[zt * sub : (zt + 1) * sub, :]

        @pl.when(jnp.logical_not(below_top))
        def _():
            for oz in range(1, nz):
                p_copy(oz, block).start()

    for o in range(1, nd):
        a_copy(o).wait_send()

    def go(which):
        pl.semaphore_signal(
            go_sem.at[which], inc=1, device_id=dev(jnp.maximum(s - 1, 0), d, z), device_id_type=MESH
        )

    if sections > 1:
        @pl.when(at_top)
        def _():
            go(0)

    scale = 1.0 / math.sqrt(width)
    x_sub = x_ref[pl.ds(sub_start, sub), :].astype(F32)
    radius_sub = jnp.sqrt(jnp.mean(x_sub * x_sub, axis=1, keepdims=True) + eps)
    lifted_sub = (x_sub / radius_sub * gain_ref[...]).astype(BF16)
    table_in = sign_rows(seed_ref[0, 0], 0, width, scale)
    inf_buf[d] = lax.dot_general(lifted_sub, table_in, NT, preferred_element_type=F32)

    def inf_copy(o):
        to = lax.rem(d + o, nd)
        return remote(inf_buf.at[d], inf_buf.at[d], inf_ss.at[o], inf_rs.at[o], dev(s, to, z))

    for o in range(1, nd):
        inf_copy(o).start()


    piece = R * R // nz
    per_seq = nd * sub // SEQS

    def spread():
        for o in range(1, nd):
            inf_copy(o).wait_recv()
        in_feat = inf_buf[...].reshape(nd * sub, R).astype(BF16)
        for zt in range(nz):
            entry = lax.broadcasted_iota(jnp.int32, (R, piece), 1) + zt * piece
            which = lax.broadcasted_iota(jnp.int32, (R, piece), 0)
            pick_in = (entry // R == which).astype(F32).astype(BF16)
            pick_buf[zt] = (entry % R == which).astype(F32).astype(BF16)
            left_buf[zt] = jnp.dot(in_feat, pick_in, preferred_element_type=F32)

    @pl.when(jnp.logical_not(at_top))
    def _():
        spread()

    if sections > 1:
        @pl.when(below_top)
        def _():
            pl.semaphore_wait(go_sem.at[1], 1)
            for o in range(nd):
                block = lax.rem(d + nd - o, nd)
                for oz in range(1, nz):
                    p_copy(oz, block).start()

    table_out = sign_rows(seed_ref[0, 1], d_start, cols, scale)

    def gp_copy(o, block):
        to = lax.rem(z + o, nz)
        return remote(
            gp_buf.at[z, block], gp_buf.at[z, block], gp_ss.at[o, block], gp_rs.at[o, block],
            dev(s, d, to),
        )

    for o in range(nd):
        block = lax.rem(d + nd - o, nd)
        summed = ps_buf[z, block].astype(F32)
        for oz in range(1, nz):
            p_copy(oz, block).wait_recv()
            summed = summed + pr_buf[lax.rem(z + nz - oz, nz), block].astype(F32)
        sig = jax.nn.sigmoid(summed)
        slope = sig * (1.0 + summed * (1.0 - sig))
        sum_buf[block] = summed
        slope_buf[block] = slope

        @pl.when(at_top)
        def _():
            if o:
                og_copy(o).wait_recv()
            else:
                ui_load().wait()
            gp_buf[z, block] = (ui_buf[block].astype(F32) * slope).astype(BF16)
            if sections > 1:
                for oz in range(1, nz):
                    gp_copy(oz, block).start()

    def up_copy(zt, source):
        return remote(
            up_buf.at[pl.ds(zt * sub, sub)], ui_buf.at[source], up_ss.at[zt], up_rs.at[source],
            dev(jnp.maximum(s - 1, 0), z, zt),
        )

    def uii_copy():
        return remote(up_buf, uii_buf, uii_ss.at[0], uii_rs.at[0], dev(jnp.maximum(s - 1, 0), d, z))

    @pl.when(at_top)
    def _():
        uii_load().wait()
        spread()

    @pl.when(jnp.logical_not(at_top))
    def _():
        for source in range(nd):
            up_copy(0, source).wait_recv()
        gp_buf[z] = (ui_buf[...].astype(F32) * slope_buf[...]).astype(BF16)

        @pl.when(lower)
        def _():
            for block in range(nd):
                for oz in range(1, nz):
                    gp_copy(oz, block).start()

    pl.semaphore_wait(far_sem.at[0], column - 1)
    grad_pre = gp_buf[z]
    plane = nd * nz
    mine = d * nz + z

    def dt_copy(o):
        to = lax.rem(mine + o, plane)
        return remote(
            dot_buf.at[mine], dot_buf.at[mine], dt_ss.at[o], dt_rs.at[o],
            dev(s, to // nz, lax.rem(to, nz)),
        )

    @pl.when(lower)
    def _():
        pre = gp_buf[z].astype(F32) * sum_buf[...]
        own_dot = jnp.sum(pre.reshape(nd * sub, cols), axis=1, keepdims=True)
        dot_buf[mine] = jnp.broadcast_to(own_dot, (tok, tok)).T[:8, :]
        for o in range(1, plane):
            dt_copy(o).start()

    out_feat = lax.dot_general(
        grad_pre.reshape(nd * sub, cols), table_out, NT, preferred_element_type=F32
    ).astype(BF16)
    for zt in range(nz):
        product = left_buf[zt] * jnp.dot(out_feat, pick_buf[zt], preferred_element_type=F32)
        for k in range(SEQS):
            g_buf[zt, k : k + 1, :] = jnp.sum(
                product[k * per_seq : (k + 1) * per_seq], axis=0, keepdims=True
            )

    def g_copy(o):
        to = lax.rem(mine + o, plane)
        return remote(
            g_buf.at[lax.rem(to, nz)], gr_buf.at[mine], g_ss.at[o], g_rs.at[o],
            dev(s, to // nz, lax.rem(to, nz)),
        )

    for o in range(1, plane):
        g_copy(o).start()
    gr_buf[mine] = g_buf[z]

    def gn_copy(o):
        to = lax.rem(d + nd - o, nd)
        return remote(gns_buf.at[to], gnr_buf.at[d], gn_ss.at[o], gn_rs.at[o], dev(s, to, z))

    @pl.when(lower)
    def _():
        for o in range(nd):
            block = lax.rem(d + nd - o, nd)
            for oz in range(1, nz):
                gp_copy(oz, block).wait_recv()
            if o == nd - 1:
                for each in range(nd):
                    for oz in range(1, nz):
                        gp_copy(oz, each).wait_send()

                @pl.when(at_top)
                def _():
                    go(1)

            rows = gp_buf[:, block].reshape(tok, cols)
            part = lax.dot_general(rows, w_ref[...], NT, preferred_element_type=F32).astype(BF16)
            if o:
                gns_buf[block] = part
                gn_copy(o).start()
            else:
                gnr_buf[d] = part
        for o in range(1, plane):
            dt_copy(o).wait_recv()
        for zt in range(nz):
            dots = dot_buf[zt]
            for dt in range(1, nd):
                dots = dots + dot_buf[dt * nz + zt]
            turn_buf[...] = jnp.broadcast_to(dots[:1, :] * (1.0 / width), (tok, tok)).T
            mean_buf[zt] = turn_buf[pl.ds(sub_start_d, sub), :]
        for o in range(1, nd):
            gn_copy(o).wait_recv()
        if sections > 2:
            @pl.when(jnp.logical_not(at_top))
            def _():
                uii_copy().wait_recv()
        for zt in range(nz):
            rows = pl.ds(zt * sub, sub)
            grad_norm = gnr_buf[0, rows].astype(F32)
            for dt in range(1, nd):
                grad_norm = grad_norm + gnr_buf[dt, rows].astype(F32)
            scaled = grad_norm.astype(BF16).astype(F32) * gain_ref[:, pl.ds(z_start, feat)]
            change = (scaled - norm_buf[rows] * mean_buf[zt][:, :1]) / rad_buf[rows, :1]
            up_buf[rows] = (uii_buf[rows].astype(F32) + change).astype(BF16)
            up_copy(zt, d).start()
        if sections > 2:
            @pl.when(s > 1)
            def _():
                uii_copy().start()

    for o in range(1, plane):
        g_copy(o).wait_recv()
    grads = gr_buf[0]
    for other in range(1, plane):
        grads = grads + gr_buf[other]
    out_ref[:, :piece] = grads
    queries = q_ref[...]
    high = grads.astype(BF16)
    rest = grads - high.astype(F32)
    middle = rest.astype(BF16)
    low = (rest - middle.astype(F32)).astype(BF16)
    part = lax.dot_general(high, queries, NT, preferred_element_type=F32)
    part = part + lax.dot_general(middle, queries, NT, preferred_element_type=F32)
    part = part + lax.dot_general(low, queries, NT, preferred_element_type=F32)
    sc_buf[here] = part

    def sc_copy(o):
        to = lax.rem(here + o, column)
        return remote(
            sc_buf.at[here], sc_buf.at[here], sc_ss.at[o], sc_rs.at[o],
            dev(to // nz, d, lax.rem(to, nz)),
        )

    for o in range(1, column):
        sc_copy(o).start()

    for o in range(1, nd):
        inf_copy(o).wait_send()
    for block in range(nd):
        for oz in range(1, nz):
            p_copy(oz, block).wait_send()

    @pl.when(at_top)
    def _():
        for o in range(1, nd):
            og_copy(o).wait_send()

    @pl.when(lower)
    def _():
        for o in range(1, plane):
            dt_copy(o).wait_send()
        for o in range(1, nd):
            gn_copy(o).wait_send()
        for zt in range(nz):
            up_copy(zt, d).wait_send()
        if sections > 2:
            @pl.when(s > 1)
            def _():
                uii_copy().wait_send()

    for o in range(1, plane):
        g_copy(o).wait_send()
    for o in range(1, column):
        sc_copy(o).wait_recv()
    scores = sc_buf[0]
    for other in range(1, column):
        scores = scores + sc_buf[other]
    out_ref[:, piece : piece + scores.shape[1]] = scores
    for o in range(1, column):
        sc_copy(o).wait_send()


def pair_kernel(
    nd, nz, lag, gap, late,
    x_hbm, w_hbm, gain_ref, seed_ref, og_ref, q_ref,
    out_ref,
    x_ref, w_ref, wide_ref, tab_in, tab_out, norm_buf, rad_buf,
    a_buf, p_buf, un_buf, uo_buf, dn_buf, do_buf,
    og_buf, uii_buf, gp_buf, dot_buf, gns_buf, gnr_buf,
    so_buf, slope_buf, tabr_buf, infs_buf, infr_buf, low_buf,
    left_buf, g_buf, gr_buf, g1_buf, gr1_buf, sc_buf,
    in_sem, go_sem, far_sem,
    a_ss, a_rs, og_ss, og_rs, up_ss, up_rs, dn_ss, dn_rs, gn_ss, gn_rs,
    so_ss, so_rs, sl_ss, sl_rs, side_ss, side_rs, g_ss, g_rs, g1_ss, g1_rs, sc_ss, sc_rs,
):
    s = lax.axis_index("section")
    d = lax.axis_index("dp")
    z = lax.axis_index("tensor")
    tok, width = x_hbm.shape
    feat = width // nz
    cols = width // nd
    sub = tok // nz
    plane = nd * nz
    column = 2 * nz
    piece = R * R // nz
    lanes = tab_out.shape[0]
    half = tok // 2
    per_seq = nd // SEQS
    at_top = s == 1
    z_start = pl.multiple_of(z * feat, feat)
    d_start = pl.multiple_of(d * cols, cols)
    here = s * nz + z
    mine = d * nz + z
    scale = 1.0 / math.sqrt(width)

    def dev(s_to, d_to, z_to):
        return {"section": s_to, "dp": d_to, "tensor": z_to}

    def flip(j):
        to, bit = d, 1
        while bit < nd:
            flag = (j // bit) % 2 if isinstance(j, int) else lax.rem(lax.div(j, bit), 2)
            to = to + flag * bit * (1 - 2 * lax.rem(lax.div(d, bit), 2))
            bit *= 2
        return to

    def remote(src, dst, ss, rs, to):
        return pltpu.make_async_remote_copy(
            src_ref=src, dst_ref=dst, send_sem=ss, recv_sem=rs, device_id=to, device_id_type=MESH
        )

    def signal(sem, to):
        pl.semaphore_signal(sem, inc=1, device_id=to, device_id_type=MESH)

    x_load = pltpu.make_async_copy(x_hbm, x_ref, in_sem.at[0])
    w_load = pltpu.make_async_copy(w_hbm, w_ref, in_sem.at[1])
    x_load.start()
    w_load.start()
    barrier = pltpu.get_barrier_semaphore()

    def signal_column(sem):
        for o in range(1, column):
            to = lax.rem(here + o, column)
            signal(sem, dev(to // nz, d, lax.rem(to, nz)))

    for j in range(1, nd):
        signal(barrier, dev(s, flip(j), z))
    signal_column(barrier)

    ui_load = pltpu.make_async_copy(og_ref.at[:, pl.ds(d_start, cols)], og_buf.at[0], in_sem.at[2])
    uii_load = pltpu.make_async_copy(og_ref.at[:, pl.ds(z_start, feat)], uii_buf, in_sem.at[3])

    @pl.when(at_top)
    def _():
        ui_load.start()
        uii_load.start()

    table_row = jnp.where(at_top, d_start, z_start)
    tab_out[:R] = sign_rows(seed_ref[0, 1], table_row, cols, scale)
    tab_out[R:] = jnp.zeros((lanes - R, cols), BF16)
    tab_in[...] = sign_rows(seed_ref[0, 0], 0, width, scale)

    x_load.wait()
    hidden = x_ref[...].astype(F32)
    radius = jnp.sqrt(jnp.mean(hidden * hidden, axis=1, keepdims=True) + eps)
    normed_z = x_ref[:, pl.ds(z_start, feat)].astype(F32) / radius
    norm_buf[...] = normed_z
    rad_buf[...] = jnp.broadcast_to(radius, rad_buf.shape)
    a_buf[0] = (normed_z * gain_ref[:, pl.ds(z_start, feat)]).astype(BF16)

    pl.semaphore_wait(barrier, nd - 1 + column - 1)

    def a_copy(j, h, via=0):
        rows = pl.ds(h * half, half)
        return remote(
            a_buf.at[via, rows], a_buf.at[j, rows], a_ss.at[0], a_rs.at[2 * j + h - 2],
            dev(s, flip(j - via), z),
        )

    def a_start():
        a_copy(1, 0).start()
        a_copy(2, 1).start()
        a_copy(1, 1).start()
        a_copy(2, 0).start()

    def a_wait(j):
        if j == 1:
            a_copy(1, 0).wait_recv()
            a_copy(3, 0, 1).start()
            a_copy(2, 1).wait_recv()
            a_copy(3, 1, 2).start()
            a_copy(1, 1).wait_recv()
        if j == 2:
            a_copy(2, 0).wait_recv()
        if j == 3:
            for h in range(2):
                a_copy(3, h).wait_recv()

    def a_sent():
        moved = a_buf.at[pl.ds(1, nd - 1)]
        remote(moved, moved, a_ss.at[0], a_rs.at[0], dev(s, flip(1), z)).wait_send()

    def og_copy(j):
        to = flip(j)
        src = og_ref.at[:, pl.ds(pl.multiple_of(to * cols, cols), cols)]
        return remote(src, og_buf.at[j], og_ss.at[0], og_rs.at[j - 1], dev(s, to, z))

    @pl.when(at_top)
    def _():
        a_start()

    signal_column(far_sem.at[0])
    w_load.wait()

    def in_features():
        lifted = (x_ref[...].astype(F32) / rad_buf[:, :1] * gain_ref[...]).astype(BF16)
        return lax.dot_general(lifted, tab_in[...], NT, preferred_element_type=F32).astype(BF16)

    def pick_in(zt):
        entry = lax.broadcasted_iota(jnp.int32, (R, piece), 1) + zt * piece
        which = lax.broadcasted_iota(jnp.int32, (R, piece), 0)
        return (entry // R == which).astype(F32).astype(BF16)

    def pick_out():
        entry = lax.broadcasted_iota(jnp.int32, (R, piece), 1)
        which = lax.broadcasted_iota(jnp.int32, (R, piece), 0)
        return (entry % R == which).astype(F32).astype(BF16)

    def up_copy(c, first):
        src = p_buf.at[c] if first else uo_buf.at[c]
        return remote(src, un_buf.at[c], up_ss.at[0], up_rs.at[c], dev(s, d, jnp.minimum(z + 1, nz - 1)))

    def dn_copy(c, first):
        src = p_buf.at[c] if first else do_buf.at[c]
        return remote(src, dn_buf.at[c], dn_ss.at[0], dn_rs.at[c], dev(s, d, jnp.maximum(z - 1, 0)))

    def gn_copy(j, row, rows, h, to):
        return remote(
            gns_buf.at[j, pl.ds(row, rows)], gnr_buf.at[j, pl.ds(row, rows)],
            gn_ss.at[0], gn_rs.at[j - 1 + h], dev(s, to, z),
        )

    def so_copy(j):
        return remote(so_buf.at[0, j], so_buf.at[1, j], so_ss.at[0], so_rs.at[j - 1], dev(0, flip(j), z))

    def slope_copy(j):
        src = so_buf.at[1, j] if j else so_buf.at[0, 0]
        return remote(src, slope_buf.at[z], sl_ss.at[0], sl_rs.at[0], dev(1, d, flip(j)))

    def slope_arrival():
        return remote(so_buf.at[0], slope_buf, sl_ss.at[0], sl_rs.at[0], dev(1 - s, d, z))

    def back(buf, j, row, rows):
        pre = gp_buf[j, pl.ds(row, rows)]
        both = jnp.dot(pre, wide_ref[...], preferred_element_type=F32)
        dot = dot_buf[j, pl.ds(row, rows)]
        high = dot.astype(BF16).astype(F32)
        lane = lax.broadcasted_iota(jnp.int32, (rows, lanes), 1)
        extra = jnp.where(lane == R, high, jnp.where(lane == R + 1, dot - high, both[:, feat:]))
        buf[j, pl.ds(row, rows), :feat] = both[:, :feat].astype(BF16)
        buf[j, pl.ds(row, rows), feat:] = extra.astype(BF16)

    def slope_of(total):
        sig = jax.nn.sigmoid(total)
        return sig * (1.0 + total * (1.0 - sig))

    lag_up = z * lag
    lag_dn = (nz - 1 - z) * lag
    lag_all = jnp.maximum(lag_up, lag_dn) + late
    slots = plane + gap + (nz - 1) * lag + late

    def chunk_at(v):
        valid = jnp.logical_and(v >= 0, v < plane + gap)
        valid = jnp.logical_and(valid, jnp.logical_or(v < nz, v >= nz + gap))
        return jnp.where(v < nz, v, v - gap), valid

    def relay(c, valid, gets, sends, copy, inbox, outbox):

        @pl.when(jnp.logical_and(valid, gets))
        def _():
            copy(c, True).wait_recv()

        @pl.when(jnp.logical_and(valid, jnp.logical_and(sends, jnp.logical_not(gets))))
        def _():
            copy(c, True).start()

        @pl.when(jnp.logical_and(valid, jnp.logical_and(sends, gets)))
        def _():
            outbox[c] = (inbox[c].astype(F32) + p_buf[c].astype(F32)).astype(BF16)
            copy(c, False).start()

    def sweep(on_block, on_total):
        def slot(i, carry):
            for j in range(nd):
                @pl.when(i == (j * nz + gap if j else 0))
                def _(j=j):
                    on_block(j)
                    multiply(j)

            c, valid = chunk_at(i - lag_up)
            relay(c, valid, z > 0, z < nz - 1, up_copy, un_buf, uo_buf)
            c, valid = chunk_at(i - lag_dn)
            relay(c, valid, z < nz - 1, z > 0, dn_copy, dn_buf, do_buf)
            c, valid = chunk_at(i - lag_all)
            q = lax.rem(jnp.maximum(c, 0), nz)
            j_now = lax.div(jnp.maximum(c, 0), nz)

            def total_of(up, dn):
                total = p_buf[c].astype(F32)
                if up:
                    total = total + un_buf[c].astype(F32)
                if dn:
                    total = total + dn_buf[c].astype(F32)
                on_total(j_now, q, total)

            @pl.when(jnp.logical_and(valid, z == 0))
            def _():
                total_of(False, True)

            @pl.when(jnp.logical_and(valid, z == nz - 1))
            def _():
                total_of(True, False)

            @pl.when(jnp.logical_and(valid, jnp.logical_and(z > 0, z < nz - 1)))
            def _():
                total_of(True, True)

            @pl.when(valid)
            def _():
                after_total(j_now, q)

            return carry

        lax.fori_loop(0, slots, slot, 0)

    def multiply(j):
        part = jnp.dot(a_buf[j], w_ref[...], preferred_element_type=F32).astype(BF16)
        for q in range(nz):
            p_buf[j * nz + q] = part[q * sub : (q + 1) * sub]

    def after_total(j, q):
        @pl.when(jnp.logical_and(q == nz - 1, j == 0))
        def _():
            back(gnr_buf, 0, 0, tok)

        @pl.when(jnp.logical_and(q == nz - 1, jnp.logical_and(j > 0, j < nd - 1)))
        def _():
            back(gns_buf, j, 0, tok)
            gn_copy(j, 0, tok, 0, flip(j)).start()

        for h in range(2):
            @pl.when(jnp.logical_and(q == (h + 1) * nz // 2 - 1, j == nd - 1))
            def _(h=h):
                back(gns_buf, nd - 1, h * half, half)
                gn_copy(nd - 1, h * half, half, h, flip(nd - 1)).start()

    def sums_sent(ss, rs, count):
        moved = p_buf.at[pl.ds(0, count)]
        remote(moved, moved, ss.at[0], rs.at[0], dev(1 - s, d, z)).wait_send()

    def g_copy(o):
        return remote(g_buf.at[o % nz], gr_buf.at[mine], g_ss.at[0], g_rs.at[0], dev(0, o // nz, o % nz))

    def g1_copy(j):
        return remote(g1_buf, gr1_buf.at[j], g1_ss.at[0], g1_rs.at[0], dev(1, flip(j), z))

    def side_copy(which):
        src, dst = ((infs_buf, infr_buf), (tab_out, tabr_buf))[which]
        return remote(src, dst, side_ss.at[which], side_rs.at[which], dev(1, d, z))

    def side_arrival(which):
        src, dst = ((infs_buf, infr_buf), (tab_out, tabr_buf))[which]
        return remote(src, dst, side_ss.at[which], side_rs.at[which], dev(0, d, z))

    def sc_copy(o):
        to = lax.rem(here + o, column)
        return remote(
            sc_buf.at[here], sc_buf.at[here], sc_ss.at[0], sc_rs.at[0], dev(to // nz, d, lax.rem(to, nz))
        )

    def score():
        grads = out_ref[:, :piece]
        queries = q_ref[...]
        high = grads.astype(BF16)
        rest = grads - high.astype(F32)
        middle = rest.astype(BF16)
        low = (rest - middle.astype(F32)).astype(BF16)
        part = lax.dot_general(high, queries, NT, preferred_element_type=F32)
        part = part + lax.dot_general(middle, queries, NT, preferred_element_type=F32)
        part = part + lax.dot_general(low, queries, NT, preferred_element_type=F32)
        sc_buf[here] = part
        for o in range(1, column):
            sc_copy(o).start()

    @pl.when(at_top)
    def _():
        def on_block(j):
            if j == 1:
                wide_ref[:, :feat] = w_ref[...].T
                wide_ref[:, feat:] = tab_out[...].T
            a_wait(j)
            if j == 1:
                signal(go_sem.at[0], dev(0, d, z))
            if j == OGA:
                og_copy(1).start()
                og_copy(2).start()
            if j == OGB:
                og_copy(3).start()

        def on_total(j, q, total):
            for each in range(nd):
                @pl.when(jnp.logical_and(q == 0, j == each))
                def _(each=each):
                    if each:
                        og_copy(each).wait_recv()
                    else:
                        ui_load.wait()

            rows = pl.ds(pl.multiple_of(q * sub, sub), sub)
            pre = (og_buf[j, rows].astype(F32) * slope_of(total)).astype(BF16)
            gp_buf[j, rows] = pre
            dot = jnp.sum(pre.astype(F32) * total, axis=1, keepdims=True)
            dot_buf[j, rows] = jnp.broadcast_to(dot, (sub, lanes))

        sweep(on_block, on_total)

        in_feat = in_features()
        g_left = jnp.dot(in_feat, pick_in(z), preferred_element_type=F32)
        left_buf[nz] = g_left
        for which in range(2):
            side_arrival(which).wait_recv()
        for zt in range(nz):
            left_buf[zt] = jnp.dot(infr_buf[:, :R], pick_in(zt), preferred_element_type=F32)
        uii_load.wait()
        pl.semaphore_wait(far_sem.at[0], column - 1)
        slope_arrival().wait_recv()
        for j in range(1, nd - 1):
            gn_copy(j, 0, tok, 0, d).wait_recv()
        for k in range(nz):
            if k * 2 % nz == 0:
                h = k * 2 // nz
                gn_copy(nd - 1, h * half, half, h, d).wait_recv()
            rows = pl.ds(k * sub, sub)
            grad_norm = gnr_buf[0, rows, :feat].astype(F32)
            extra = gnr_buf[0, rows, feat:].astype(F32)
            for j in range(1, nd):
                grad_norm = grad_norm + gnr_buf[j, rows, :feat].astype(F32)
                extra = extra + gnr_buf[j, rows, feat:].astype(F32)
            dot_buf[0, rows] = extra
            mean_dot = (extra[:, R : R + 1] + extra[:, R + 1 : R + 2]) * (1.0 / width)
            scaled = grad_norm.astype(BF16).astype(F32) * gain_ref[:, pl.ds(z_start, feat)]
            change = (scaled - norm_buf[rows] * mean_dot) / rad_buf[rows, :1]
            upstream = (uii_buf[rows].astype(F32) + change).astype(BF16)
            low_buf[rows] = (upstream.astype(F32) * slope_buf[k].astype(F32)).astype(BF16)
        out_low = lax.dot_general(low_buf[...], tabr_buf[...], NT, preferred_element_type=F32)
        spread = pick_out()
        right = jnp.dot(out_low[:, :R].astype(BF16), spread, preferred_element_type=F32)
        for zt in range(nz):
            g_buf[zt] = jnp.sum(left_buf[zt] * right, axis=0, keepdims=True)
        for o in range(plane):
            g_copy(o).start()

        right = jnp.dot(dot_buf[0, :, :R].astype(BF16), spread, preferred_element_type=F32)
        own = jnp.sum(left_buf[nz] * right, axis=0, keepdims=True)
        g1_buf[...] = own
        for j in range(1, nd):
            g1_copy(j).start()
        gr1_buf[0] = own
        moved = gr1_buf.at[pl.ds(1, nd - 1)]
        remote(moved, moved, g1_ss.at[0], g1_rs.at[0], dev(0, d, z)).wait_recv()
        for k in range(SEQS):
            row = jnp.zeros((1, piece), F32)
            for group in range(SEQS):
                held = gr1_buf[group * per_seq]
                for j in range(group * per_seq + 1, (group + 1) * per_seq):
                    held = held + gr1_buf[j]
                row = row + jnp.where(lax.div(flip(group * per_seq), per_seq) == k, held, 0.0)
            out_ref[k : k + 1, :piece] = row
        score()
        moved = gns_buf.at[pl.ds(1, nd - 1)]
        remote(moved, moved, gn_ss.at[0], gn_rs.at[0], dev(0, d, z)).wait_send()
        moved = og_buf.at[pl.ds(1, nd - 1)]
        remote(moved, moved, og_ss.at[0], og_rs.at[0], dev(0, d, z)).wait_send()
        moved = gr1_buf.at[pl.ds(1, nd - 1)]
        remote(moved, moved, g1_ss.at[0], g1_rs.at[0], dev(0, d, z)).wait_send()
        remote(gr_buf, gr_buf, g_ss.at[0], g_rs.at[0], dev(0, d, z)).wait_send()
        a_sent()

        @pl.when(z < nz - 1)
        def _():
            sums_sent(up_ss, up_rs, plane)

        @pl.when(z > 0)
        def _():
            sums_sent(dn_ss, dn_rs, plane)


    @pl.when(jnp.logical_not(at_top))
    def _():
        low = z < nz // 2
        outer = jnp.logical_or(z == 0, z == nz - 1)
        inner_z = jnp.where(low, 1, nz - 2)
        outer_z = jnp.where(low, 0, nz - 1)

        def lift(src, c, to):
            return remote(src, un_buf.at[c], up_ss.at[0], up_rs.at[c], dev(0, d, to))

        def drop(src, c, to):
            return remote(src, dn_buf.at[c], dn_ss.at[0], dn_rs.at[c], dev(0, d, to))

        def hand_on(block):
            for o in range(1, nz):
                c = block * nz + jnp.where(low, nz - o, o - 1)

                @pl.when(jnp.logical_and(outer, low))
                def _(c=c):
                    lift(p_buf.at[c], c, inner_z).start()

                @pl.when(jnp.logical_and(outer, jnp.logical_not(low)))
                def _(c=c):
                    drop(p_buf.at[c], c, inner_z).start()

            c = block * nz + outer_z

            @pl.when(jnp.logical_and(jnp.logical_not(outer), low))
            def _():
                lift(p_buf.at[c], c, outer_z).start()

            @pl.when(jnp.logical_and(jnp.logical_not(outer), jnp.logical_not(low)))
            def _():
                drop(p_buf.at[c], c, outer_z).start()

        def pass_on(block):
            for o in range(nz // 2):
                to = jnp.where(low, nz - 1 - o, o)
                c = block * nz + to

                @pl.when(jnp.logical_and(jnp.logical_not(outer), low))
                def _(c=c, to=to):
                    lift(p_buf.at[c], c, to).wait_recv()
                    uo_buf[c] = (un_buf[c].astype(F32) + p_buf[c].astype(F32)).astype(BF16)
                    lift(uo_buf.at[c], c, to).start()

                @pl.when(jnp.logical_and(jnp.logical_not(outer), jnp.logical_not(low)))
                def _(c=c, to=to):
                    drop(p_buf.at[c], c, to).wait_recv()
                    uo_buf[c] = (dn_buf[c].astype(F32) + p_buf[c].astype(F32)).astype(BF16)
                    drop(uo_buf.at[c], c, to).start()

        def lower_slope(block):
            c = block * nz + z
            lift(p_buf.at[c], c, z).wait_recv()
            drop(p_buf.at[c], c, z).wait_recv()
            total = p_buf[c].astype(F32) + un_buf[c].astype(F32) + dn_buf[c].astype(F32)
            so_buf[0, block] = slope_of(total).astype(BF16)
            if block:
                so_copy(block).start()
            else:
                slope_copy(0).start()

        def forward(block):
            so_copy(block).wait_recv()
            slope_copy(block).start()

        multiply(0)
        hand_on(0)
        infs_buf[:, :R] = in_features()
        infs_buf[:, R:] = jnp.zeros((tok, lanes - R), BF16)
        for which in range(2):
            side_copy(which).start()
        pl.semaphore_wait(go_sem.at[0], 1)
        a_start()
        pl.semaphore_wait(far_sem.at[0], column - 1)
        pass_on(0)
        lower_slope(0)
        for block in range(1, nd):
            a_wait(block)
            multiply(block)
            hand_on(block)
        pass_on(1)
        for block in range(2, nd):
            pass_on(block)
            lower_slope(block - 1)
            if block > 2:
                forward(block - 2)
        lower_slope(nd - 1)
        for block in range(nd - 2, nd):
            forward(block)
        remote(gr_buf, gr_buf, g_ss.at[0], g_rs.at[0], dev(1, d, z)).wait_recv()
        for k in range(SEQS):
            held = gr_buf[k * per_seq * nz]
            for o in range(k * per_seq * nz + 1, (k + 1) * per_seq * nz):
                held = held + gr_buf[o]
            out_ref[k : k + 1, :piece] = held
        score()
        a_sent()
        moved = so_buf.at[0, pl.ds(1, nd - 1)]
        remote(moved, moved, so_ss.at[0], so_rs.at[0], dev(1, d, z)).wait_send()
        slope_arrival().wait_send()
        for which in range(2):
            side_copy(which).wait_send()
        @pl.when(low)
        def _():
            sums_sent(up_ss, up_rs, nd * (nz - 1))

        @pl.when(jnp.logical_not(low))
        def _():
            sums_sent(dn_ss, dn_rs, nd * (nz - 1))

    moved = sc_buf.at[pl.ds(0, column - 1)]
    others = remote(moved, moved, sc_ss.at[0], sc_rs.at[0], dev(1 - s, d, z))
    others.wait_recv()
    scores = sc_buf[0]
    for other in range(1, column):
        scores = scores + sc_buf[other]
    out_ref[:, piece : piece + scores.shape[1]] = scores
    others.wait_send()


def pair_call(nd, nz, tok, width, queries):
    feat, cols, sub, plane, column = width // nz, width // nd, tok // nz, nd * nz, 2 * nz
    piece, lanes = R * R // nz, 2 * R
    dma = pltpu.SemaphoreType.DMA
    sems = []
    for arrivals in (2 * nd - 2, nd - 1, plane, plane, nd, nd - 1, 1):
        sems += [dma((1,)), dma((arrivals,))]
    sems += [dma((2,)), dma((2,))]
    for _ in range(3):
        sems += [dma((1,)), dma((1,))]
    vmem = pl.BlockSpec(memory_space=pltpu.VMEM)
    hbm = pl.BlockSpec(memory_space=pl.ANY)
    chunks = pltpu.VMEM((plane, sub, cols), BF16)
    blocks = pltpu.VMEM((nd, tok, cols), BF16)
    return pl.pallas_call(
        functools.partial(pair_kernel, nd, nz, LAG, GAP, LATE),
        out_shape=pltpu.VMEM((SEQS, piece + queries), F32),
        in_specs=[hbm, hbm, vmem, pl.BlockSpec(memory_space=pltpu.SMEM), hbm, vmem],
        out_specs=vmem,
        scratch_shapes=[
            pltpu.VMEM((tok, width), BF16),
            pltpu.VMEM((feat, cols), BF16),
            pltpu.VMEM((cols, feat + lanes), BF16),
            pltpu.VMEM((R, width), BF16),
            pltpu.VMEM((lanes, cols), BF16),
            pltpu.VMEM((tok, feat), F32),
            pltpu.VMEM((tok, 128), F32),
            blocks, chunks, chunks, chunks, chunks, chunks,
            blocks,
            pltpu.VMEM((tok, feat), BF16),
            blocks,
            pltpu.VMEM((nd, tok, lanes), F32),
            pltpu.VMEM((nd, tok, feat + lanes), BF16),
            pltpu.VMEM((nd, tok, feat + lanes), BF16),
            pltpu.VMEM((2, nd, sub, cols), BF16),
            pltpu.VMEM((nz, sub, cols), BF16),
            pltpu.VMEM((lanes, cols), BF16),
            pltpu.VMEM((tok, lanes), BF16),
            pltpu.VMEM((tok, lanes), BF16),
            pltpu.VMEM((tok, cols), BF16),
            pltpu.VMEM((nz + 1, tok, piece), F32),
            pltpu.VMEM((nz, 1, piece), F32),
            pltpu.VMEM((plane, 1, piece), F32),
            pltpu.VMEM((1, piece), F32),
            pltpu.VMEM((nd, 1, piece), F32),
            pltpu.VMEM((column, SEQS, queries), F32),
            dma((4,)),
            pltpu.SemaphoreType.REGULAR((1,)),
            pltpu.SemaphoreType.REGULAR((1,)),
            *sems,
        ],
        compiler_params=pltpu.CompilerParams(
            collective_id=0, has_side_effects=True, vmem_limit_bytes=60 * 1024 * 1024
        ),
    )


def stack_call(sections, nd, nz, tok, width, queries):
    feat, cols = width // nz, width // nd
    sub = tok // nz
    piece = R * R // nz
    column = sections * nz
    plane = nd * nz
    vmem = pl.BlockSpec(memory_space=pltpu.VMEM)
    hbm = pl.BlockSpec(memory_space=pl.ANY)
    dma = pltpu.SemaphoreType.DMA
    sems = []
    for shape in ((nd,), (nd,), (nz, nd), (nd,), (nz, nd), (nd,), (plane,)):
        sems += [dma(shape), dma(shape)]
    sems += [dma((nz,)), dma((nd,)), dma((1,)), dma((1,))]
    sems += [dma((plane,)), dma((plane,)), dma((column,)), dma((column,))]
    return pl.pallas_call(
        functools.partial(kernel, sections, nd, nz),
        out_shape=jax.ShapeDtypeStruct((SEQS, piece + queries), F32),
        in_specs=[hbm, hbm, vmem, pl.BlockSpec(memory_space=pltpu.SMEM), hbm, vmem],
        out_specs=vmem,
        scratch_shapes=[
            pltpu.VMEM((nd, tok, feat), BF16),
            pltpu.VMEM((nd, sub, R), F32),
            pltpu.VMEM((nz, nd, sub, cols), BF16),
            pltpu.VMEM((nz, nd, sub, cols), BF16),
            pltpu.VMEM((nd, sub, cols), F32),
            pltpu.VMEM((nd, sub, cols), BF16),
            pltpu.VMEM((tok, feat), BF16),
            pltpu.VMEM((nz, nd, sub, cols), BF16),
            pltpu.VMEM((nd, tok, feat), BF16),
            pltpu.VMEM((nd, tok, feat), BF16),
            pltpu.VMEM((plane, 8, tok), F32),
            pltpu.VMEM((tok, feat), BF16),
            pltpu.VMEM((nz, SEQS, piece), F32),
            pltpu.VMEM((plane, SEQS, piece), F32),
            pltpu.VMEM((column, SEQS, queries), F32),
            pltpu.VMEM((tok, width), BF16),
            pltpu.VMEM((feat, cols), BF16),
            pltpu.VMEM((nd, sub, cols), F32),
            pltpu.VMEM((tok, feat), F32),
            pltpu.VMEM((tok, 128), F32),
            pltpu.VMEM((tok, tok), F32),
            pltpu.VMEM((nz, sub, tok), F32),
            pltpu.VMEM((nz, tok, piece), F32),
            pltpu.VMEM((nz, R, piece), BF16),
            *sems,
            dma((4,)),
            pltpu.SemaphoreType.REGULAR((2,)),
            pltpu.SemaphoreType.REGULAR((1,)),
        ],
        compiler_params=pltpu.CompilerParams(
            collective_id=0, has_side_effects=True, vmem_limit_bytes=60 * 1024 * 1024
        ),
    )


def part_outputs(both_ref, grads_ref, scores_ref):
    piece = grads_ref.shape[1]
    grads_ref[...] = both_ref[:, :piece]
    scores_ref[...] = both_ref[:, piece : piece + scores_ref.shape[1]]


def body(section_input, weights, gains, proj_seeds, out_grad, query_grads):
    sections = lax.axis_size("section")
    nd = lax.axis_size("dp")
    nz = lax.axis_size("tensor")
    tok, width = section_input.shape[1:]
    feat = weights.shape[1]
    cols = weights.shape[2]
    assert nd == nz and feat == cols
    piece = R * R // nz
    queries = query_grads.shape[1]
    vmem = pl.BlockSpec(memory_space=pltpu.VMEM)
    paired = sections == 2 and nd == 4 and nz == 4
    if paired:
        call = pair_call(nd, nz, tok, width, queries)
    else:
        call = stack_call(sections, nd, nz, tok, width, queries)
    out = call(section_input[0], weights[0], gains, proj_seeds, out_grad, query_grads[0])
    if paired:
        out = pltpu.with_memory_space_constraint(out, pltpu.VMEM)
    grads, scores = pl.pallas_call(
        part_outputs,
        out_shape=(
            jax.ShapeDtypeStruct((SEQS, piece), F32),
            jax.ShapeDtypeStruct((SEQS, queries), F32),
        ),
        in_specs=[vmem],
        out_specs=(vmem, vmem),
    )(out)
    return (grads[None], scores)


def solution(mesh):
    in_specs = (
        P("section", "dp", None),
        P("section", "tensor", "dp"),
        P("section", None),
        P("section", None),
        P("dp", None),
        P("section", "dp", "tensor"),
    )
    out_specs = (P("section", None, "tensor"), P(None, "dp"))
    return jax.shard_map(body, mesh=mesh, in_specs=in_specs, out_specs=out_specs, check_vma=False)
```

```python
import functools
import math

import jax
import jax.numpy as jnp
from jax import lax
from jax.experimental import pallas as pl
from jax.experimental.pallas import tpu as pltpu
from jax.sharding import PartitionSpec as P

R = 64
SEQS = 2
eps = 1e-05
F32 = jnp.float32
BF16 = jnp.bfloat16
MESH = pl.DeviceIdType.MESH
NT = (((1,), (1,)), ((), ()))
LAG = 6
GAP = 3
LOADS = 4


def sign_rows(seed_value, row_start, row_count, scale):
    row_index = lax.broadcasted_iota(jnp.int32, (R, row_count), 1) + row_start
    col_index = lax.broadcasted_iota(jnp.int32, (R, row_count), 0)
    mixing = row_index * 40503 + col_index * 9973 + (seed_value * 7919 + 12345)
    mixing = mixing ^ (mixing >> 13)
    mixing = mixing * 1274126177
    mixing = mixing ^ (mixing >> 16)
    parity = (mixing >> 10) & 1
    return jnp.where(parity == 1, scale, -scale).astype(BF16)


def kernel(
    sections, nd, nz,
    x_hbm, w_hbm, gain_ref, seed_ref, og_ref, q_ref,
    out_ref,
    a_buf, inf_buf, ps_buf, pr_buf, slope_buf, ui_buf, uii_buf, gp_buf,
    gns_buf, gnr_buf, dot_buf, up_buf, g_buf, gr_buf, sc_buf,
    x_ref, w_ref, sum_buf, norm_buf, rad_buf, turn_buf, mean_buf, left_buf, pick_buf,
    a_ss, a_rs, inf_ss, inf_rs, p_ss, p_rs, og_ss, og_rs, gp_ss, gp_rs,
    gn_ss, gn_rs, dt_ss, dt_rs, up_ss, up_rs, uii_ss, uii_rs,
    g_ss, g_rs, sc_ss, sc_rs, in_sem, go_sem, far_sem,
):
    s = lax.axis_index("section")
    d = lax.axis_index("dp")
    z = lax.axis_index("tensor")
    tok, width = x_hbm.shape
    feat = width // nz
    cols = width // nd
    sub = tok // nz
    at_top = s == sections - 1
    below_top = s == sections - 2
    lower = s > 0
    z_start = pl.multiple_of(z * feat, feat)
    d_start = pl.multiple_of(d * cols, cols)
    sub_start = pl.multiple_of(z * sub, sub)
    sub_start_d = pl.multiple_of(d * sub, sub)

    def dev(s_to, d_to, z_to):
        return {"section": s_to, "dp": d_to, "tensor": z_to}

    def remote(src, dst, ss, rs, to):
        return pltpu.make_async_remote_copy(
            src_ref=src, dst_ref=dst, send_sem=ss, recv_sem=rs, device_id=to, device_id_type=MESH
        )

    x_load = pltpu.make_async_copy(x_hbm, x_ref, in_sem.at[0])
    w_load = pltpu.make_async_copy(w_hbm, w_ref, in_sem.at[1])
    x_load.start()
    w_load.start()

    barrier = pltpu.get_barrier_semaphore()
    column = sections * nz
    here = s * nz + z

    def signal_column(sem):
        for o in range(1, column):
            to = lax.rem(here + o, column)
            pl.semaphore_signal(
                sem, inc=1, device_id=dev(to // nz, d, lax.rem(to, nz)), device_id_type=MESH
            )

    for o in range(1, nd):
        pl.semaphore_signal(
            barrier, inc=1, device_id=dev(s, lax.rem(d + o, nd), z), device_id_type=MESH
        )
    signal_column(barrier)

    x_load.wait()
    hidden = x_ref[...].astype(F32)
    radius = jnp.sqrt(jnp.mean(hidden * hidden, axis=1, keepdims=True) + eps)
    gain_z = gain_ref[:, pl.ds(z_start, feat)]
    normed_z = x_ref[:, pl.ds(z_start, feat)].astype(F32) / radius
    norm_buf[...] = normed_z
    rad_buf[...] = jnp.broadcast_to(radius, rad_buf.shape)
    a_buf[d] = (normed_z * gain_z).astype(BF16)

    pl.semaphore_wait(barrier, nd - 1 + column - 1)

    def a_copy(o):
        to = lax.rem(d + o, nd)
        return remote(a_buf.at[d], a_buf.at[d], a_ss.at[o], a_rs.at[o], dev(s, to, z))

    @pl.when(jnp.logical_not(below_top))
    def _():
        for o in range(1, nd):
            a_copy(o).start()

    def og_copy(o):
        to = lax.rem(d + o, nd)
        src = og_ref.at[pl.ds(sub_start, sub), pl.ds(pl.multiple_of(to * cols, cols), cols)]
        return remote(src, ui_buf.at[d], og_ss.at[o], og_rs.at[o], dev(s, to, z))

    def ui_load():
        src = og_ref.at[pl.ds(sub_start, sub), pl.ds(d_start, cols)]
        return pltpu.make_async_copy(src, ui_buf.at[d], in_sem.at[2])

    def uii_load():
        return pltpu.make_async_copy(og_ref.at[:, pl.ds(z_start, feat)], uii_buf, in_sem.at[3])

    @pl.when(at_top)
    def _():
        for o in range(1, nd):
            og_copy(o).start()
        ui_load().start()
        uii_load().start()

    @pl.when(below_top)
    def _():
        pl.semaphore_wait(go_sem.at[0], 1)
        for o in range(1, nd):
            a_copy(o).start()

    signal_column(far_sem.at[0])

    w_load.wait()

    def p_copy(o, block):
        to = lax.rem(z + o, nz)
        return remote(
            ps_buf.at[to, block], pr_buf.at[z, block], p_ss.at[o, block], p_rs.at[o, block],
            dev(s, d, to),
        )

    for o in range(nd):
        block = lax.rem(d + nd - o, nd)
        if o:
            a_copy(o).wait_recv()
        part = jnp.dot(a_buf[block], w_ref[...], preferred_element_type=F32).astype(BF16)
        for zt in range(nz):
            ps_buf[zt, block] = part[zt * sub : (zt + 1) * sub, :]

        @pl.when(jnp.logical_not(below_top))
        def _():
            for oz in range(1, nz):
                p_copy(oz, block).start()

    for o in range(1, nd):
        a_copy(o).wait_send()

    def go(which):
        pl.semaphore_signal(
            go_sem.at[which], inc=1, device_id=dev(jnp.maximum(s - 1, 0), d, z), device_id_type=MESH
        )

    if sections > 1:
        @pl.when(at_top)
        def _():
            go(0)

    scale = 1.0 / math.sqrt(width)
    x_sub = x_ref[pl.ds(sub_start, sub), :].astype(F32)
    radius_sub = jnp.sqrt(jnp.mean(x_sub * x_sub, axis=1, keepdims=True) + eps)
    lifted_sub = (x_sub / radius_sub * gain_ref[...]).astype(BF16)
    table_in = sign_rows(seed_ref[0, 0], 0, width, scale)
    inf_buf[d] = lax.dot_general(lifted_sub, table_in, NT, preferred_element_type=F32)

    def inf_copy(o):
        to = lax.rem(d + o, nd)
        return remote(inf_buf.at[d], inf_buf.at[d], inf_ss.at[o], inf_rs.at[o], dev(s, to, z))

    for o in range(1, nd):
        inf_copy(o).start()


    piece = R * R // nz
    per_seq = nd * sub // SEQS

    def spread():
        for o in range(1, nd):
            inf_copy(o).wait_recv()
        in_feat = inf_buf[...].reshape(nd * sub, R).astype(BF16)
        for zt in range(nz):
            entry = lax.broadcasted_iota(jnp.int32, (R, piece), 1) + zt * piece
            which = lax.broadcasted_iota(jnp.int32, (R, piece), 0)
            pick_in = (entry // R == which).astype(F32).astype(BF16)
            pick_buf[zt] = (entry % R == which).astype(F32).astype(BF16)
            left_buf[zt] = jnp.dot(in_feat, pick_in, preferred_element_type=F32)

    @pl.when(jnp.logical_not(at_top))
    def _():
        spread()

    if sections > 1:
        @pl.when(below_top)
        def _():
            pl.semaphore_wait(go_sem.at[1], 1)
            for o in range(nd):
                block = lax.rem(d + nd - o, nd)
                for oz in range(1, nz):
                    p_copy(oz, block).start()

    table_out = sign_rows(seed_ref[0, 1], d_start, cols, scale)

    def gp_copy(o, block):
        to = lax.rem(z + o, nz)
        return remote(
            gp_buf.at[z, block], gp_buf.at[z, block], gp_ss.at[o, block], gp_rs.at[o, block],
            dev(s, d, to),
        )

    for o in range(nd):
        block = lax.rem(d + nd - o, nd)
        summed = ps_buf[z, block].astype(F32)
        for oz in range(1, nz):
            p_copy(oz, block).wait_recv()
            summed = summed + pr_buf[lax.rem(z + nz - oz, nz), block].astype(F32)
        sig = jax.nn.sigmoid(summed)
        slope = sig * (1.0 + summed * (1.0 - sig))
        sum_buf[block] = summed
        slope_buf[block] = slope

        @pl.when(at_top)
        def _():
            if o:
                og_copy(o).wait_recv()
            else:
                ui_load().wait()
            gp_buf[z, block] = (ui_buf[block].astype(F32) * slope).astype(BF16)
            if sections > 1:
                for oz in range(1, nz):
                    gp_copy(oz, block).start()

    def up_copy(zt, source):
        return remote(
            up_buf.at[pl.ds(zt * sub, sub)], ui_buf.at[source], up_ss.at[zt], up_rs.at[source],
            dev(jnp.maximum(s - 1, 0), z, zt),
        )

    def uii_copy():
        return remote(up_buf, uii_buf, uii_ss.at[0], uii_rs.at[0], dev(jnp.maximum(s - 1, 0), d, z))

    @pl.when(at_top)
    def _():
        uii_load().wait()
        spread()

    @pl.when(jnp.logical_not(at_top))
    def _():
        for source in range(nd):
            up_copy(0, source).wait_recv()
        gp_buf[z] = (ui_buf[...].astype(F32) * slope_buf[...]).astype(BF16)

        @pl.when(lower)
        def _():
            for block in range(nd):
                for oz in range(1, nz):
                    gp_copy(oz, block).start()

    pl.semaphore_wait(far_sem.at[0], column - 1)
    grad_pre = gp_buf[z]
    plane = nd * nz
    mine = d * nz + z

    def dt_copy(o):
        to = lax.rem(mine + o, plane)
        return remote(
            dot_buf.at[mine], dot_buf.at[mine], dt_ss.at[o], dt_rs.at[o],
            dev(s, to // nz, lax.rem(to, nz)),
        )

    @pl.when(lower)
    def _():
        pre = gp_buf[z].astype(F32) * sum_buf[...]
        own_dot = jnp.sum(pre.reshape(nd * sub, cols), axis=1, keepdims=True)
        dot_buf[mine] = jnp.broadcast_to(own_dot, (tok, tok)).T[:8, :]
        for o in range(1, plane):
            dt_copy(o).start()

    out_feat = lax.dot_general(
        grad_pre.reshape(nd * sub, cols), table_out, NT, preferred_element_type=F32
    ).astype(BF16)
    for zt in range(nz):
        product = left_buf[zt] * jnp.dot(out_feat, pick_buf[zt], preferred_element_type=F32)
        for k in range(SEQS):
            g_buf[zt, k : k + 1, :] = jnp.sum(
                product[k * per_seq : (k + 1) * per_seq], axis=0, keepdims=True
            )

    def g_copy(o):
        to = lax.rem(mine + o, plane)
        return remote(
            g_buf.at[lax.rem(to, nz)], gr_buf.at[mine], g_ss.at[o], g_rs.at[o],
            dev(s, to // nz, lax.rem(to, nz)),
        )

    for o in range(1, plane):
        g_copy(o).start()
    gr_buf[mine] = g_buf[z]

    def gn_copy(o):
        to = lax.rem(d + nd - o, nd)
        return remote(gns_buf.at[to], gnr_buf.at[d], gn_ss.at[o], gn_rs.at[o], dev(s, to, z))

    @pl.when(lower)
    def _():
        for o in range(nd):
            block = lax.rem(d + nd - o, nd)
            for oz in range(1, nz):
                gp_copy(oz, block).wait_recv()
            if o == nd - 1:
                for each in range(nd):
                    for oz in range(1, nz):
                        gp_copy(oz, each).wait_send()

                @pl.when(at_top)
                def _():
                    go(1)

            rows = gp_buf[:, block].reshape(tok, cols)
            part = lax.dot_general(rows, w_ref[...], NT, preferred_element_type=F32).astype(BF16)
            if o:
                gns_buf[block] = part
                gn_copy(o).start()
            else:
                gnr_buf[d] = part
        for o in range(1, plane):
            dt_copy(o).wait_recv()
        for zt in range(nz):
            dots = dot_buf[zt]
            for dt in range(1, nd):
                dots = dots + dot_buf[dt * nz + zt]
            turn_buf[...] = jnp.broadcast_to(dots[:1, :] * (1.0 / width), (tok, tok)).T
            mean_buf[zt] = turn_buf[pl.ds(sub_start_d, sub), :]
        for o in range(1, nd):
            gn_copy(o).wait_recv()
        if sections > 2:
            @pl.when(jnp.logical_not(at_top))
            def _():
                uii_copy().wait_recv()
        for zt in range(nz):
            rows = pl.ds(zt * sub, sub)
            grad_norm = gnr_buf[0, rows].astype(F32)
            for dt in range(1, nd):
                grad_norm = grad_norm + gnr_buf[dt, rows].astype(F32)
            scaled = grad_norm.astype(BF16).astype(F32) * gain_ref[:, pl.ds(z_start, feat)]
            change = (scaled - norm_buf[rows] * mean_buf[zt][:, :1]) / rad_buf[rows, :1]
            up_buf[rows] = (uii_buf[rows].astype(F32) + change).astype(BF16)
            up_copy(zt, d).start()
        if sections > 2:
            @pl.when(s > 1)
            def _():
                uii_copy().start()

    for o in range(1, plane):
        g_copy(o).wait_recv()
    grads = gr_buf[0]
    for other in range(1, plane):
        grads = grads + gr_buf[other]
    out_ref[:, :piece] = grads
    queries = q_ref[...]
    high = grads.astype(BF16)
    rest = grads - high.astype(F32)
    middle = rest.astype(BF16)
    low = (rest - middle.astype(F32)).astype(BF16)
    part = lax.dot_general(high, queries, NT, preferred_element_type=F32)
    part = part + lax.dot_general(middle, queries, NT, preferred_element_type=F32)
    part = part + lax.dot_general(low, queries, NT, preferred_element_type=F32)
    sc_buf[here] = part

    def sc_copy(o):
        to = lax.rem(here + o, column)
        return remote(
            sc_buf.at[here], sc_buf.at[here], sc_ss.at[o], sc_rs.at[o],
            dev(to // nz, d, lax.rem(to, nz)),
        )

    for o in range(1, column):
        sc_copy(o).start()

    for o in range(1, nd):
        inf_copy(o).wait_send()
    for block in range(nd):
        for oz in range(1, nz):
            p_copy(oz, block).wait_send()

    @pl.when(at_top)
    def _():
        for o in range(1, nd):
            og_copy(o).wait_send()

    @pl.when(lower)
    def _():
        for o in range(1, plane):
            dt_copy(o).wait_send()
        for o in range(1, nd):
            gn_copy(o).wait_send()
        for zt in range(nz):
            up_copy(zt, d).wait_send()
        if sections > 2:
            @pl.when(s > 1)
            def _():
                uii_copy().wait_send()

    for o in range(1, plane):
        g_copy(o).wait_send()
    for o in range(1, column):
        sc_copy(o).wait_recv()
    scores = sc_buf[0]
    for other in range(1, column):
        scores = scores + sc_buf[other]
    out_ref[:, piece : piece + scores.shape[1]] = scores
    for o in range(1, column):
        sc_copy(o).wait_send()


def pair_kernel(
    nd, nz, lag, gap,
    x_hbm, w_hbm, gain_hbm, seed_ref, og_ref, q_hbm,
    out_ref,
    x_ref, w_ref, gain_ref, q_ref, wide_ref, tab_in, tab_out, norm_buf, rad_buf,
    a_buf, p_buf, un_buf, uo_buf, dn_buf, do_buf,
    og_buf, uii_buf, gp_buf, dot_buf, gns_buf, gnr_buf,
    so_buf, slope_buf, tabr_buf, infs_buf, infr_buf, low_buf,
    left_buf, g_buf, gr_buf, g1_buf, gr1_buf, sc_buf,
    in_sem, go_sem, far_sem,
    a_ss, a_rs, og_ss, og_rs, up_ss, up_rs, dn_ss, dn_rs, gn_ss, gn_rs,
    so_ss, so_rs, sl_ss, sl_rs, side_ss, side_rs, g_ss, g_rs, g1_ss, g1_rs, sc_ss, sc_rs,
):
    s = lax.axis_index("section")
    d = lax.axis_index("dp")
    z = lax.axis_index("tensor")
    tok, width = x_hbm.shape
    feat = width // nz
    cols = width // nd
    sub = tok // nz
    plane = nd * nz
    column = 2 * nz
    piece = R * R // nz
    lanes = tab_out.shape[0]
    half = tok // 2
    per_seq = nd // SEQS
    at_top = s == 1
    z_start = pl.multiple_of(z * feat, feat)
    d_start = pl.multiple_of(d * cols, cols)
    here = s * nz + z
    mine = d * nz + z
    scale = 1.0 / math.sqrt(width)

    def dev(s_to, d_to, z_to):
        return {"section": s_to, "dp": d_to, "tensor": z_to}

    def flip(j):
        to, bit = d, 1
        while bit < nd:
            flag = (j // bit) % 2 if isinstance(j, int) else lax.rem(lax.div(j, bit), 2)
            to = to + flag * bit * (1 - 2 * lax.rem(lax.div(d, bit), 2))
            bit *= 2
        return to

    def remote(src, dst, ss, rs, to):
        return pltpu.make_async_remote_copy(
            src_ref=src, dst_ref=dst, send_sem=ss, recv_sem=rs, device_id=to, device_id_type=MESH
        )

    def signal(sem, to):
        pl.semaphore_signal(sem, inc=1, device_id=to, device_id_type=MESH)

    x_load = pltpu.make_async_copy(x_hbm, x_ref, in_sem.at[0])
    w_load = pltpu.make_async_copy(w_hbm, w_ref, in_sem.at[1])

    def load(hbm, ref, sem, parts):
        rows = hbm.shape[0] // parts
        for part in range(parts):
            span = pl.ds(part * rows, rows)
            pltpu.make_async_copy(hbm.at[span], ref.at[span], sem).start()

    gain_load = pltpu.make_async_copy(gain_hbm, gain_ref, in_sem.at[4])
    q_load = pltpu.make_async_copy(q_hbm, q_ref, in_sem.at[5])
    load(x_hbm, x_ref, in_sem.at[0], LOADS)
    gain_load.start()
    load(w_hbm, w_ref, in_sem.at[1], LOADS)
    barrier = pltpu.get_barrier_semaphore()

    def signal_column(sem):
        for o in range(1, column):
            to = lax.rem(here + o, column)
            signal(sem, dev(to // nz, d, lax.rem(to, nz)))

    for j in range(1, nd):
        signal(barrier, dev(s, flip(j), z))
    signal_column(barrier)

    ui_load = pltpu.make_async_copy(og_ref.at[:, pl.ds(d_start, cols)], og_buf.at[0], in_sem.at[2])
    uii_load = pltpu.make_async_copy(og_ref.at[:, pl.ds(z_start, feat)], uii_buf, in_sem.at[3])

    table_row = jnp.where(at_top, d_start, z_start)
    tab_out[:R] = sign_rows(seed_ref[0, 1], table_row, cols, scale)
    tab_out[R:] = jnp.zeros((lanes - R, cols), BF16)
    x_load.wait()
    gain_load.wait()
    hidden = x_ref[...].astype(F32)
    radius = jnp.sqrt(jnp.mean(hidden * hidden, axis=1, keepdims=True) + eps)
    normed_z = x_ref[:, pl.ds(z_start, feat)].astype(F32) / radius
    norm_buf[...] = normed_z
    rad_buf[...] = jnp.broadcast_to(radius, rad_buf.shape)
    a_buf[0] = (normed_z * gain_ref[:, pl.ds(z_start, feat)]).astype(BF16)

    pl.semaphore_wait(barrier, nd - 1 + column - 1)

    def a_copy(j, h, via=0):
        rows = pl.ds(h * half, half)
        return remote(
            a_buf.at[via, rows], a_buf.at[j, rows], a_ss.at[0], a_rs.at[2 * j + h - 2],
            dev(s, flip(j - via), z),
        )

    def a_start():
        a_copy(1, 0).start()
        a_copy(2, 1).start()
        a_copy(1, 1).start()
        a_copy(2, 0).start()

    def a_wait(j):
        if j == 1:
            a_copy(1, 0).wait_recv()
            a_copy(3, 0, 1).start()
            a_copy(2, 1).wait_recv()
            a_copy(3, 1, 2).start()
            a_copy(1, 1).wait_recv()
        if j == 2:
            a_copy(2, 0).wait_recv()
        if j == 3:
            for h in range(2):
                a_copy(3, h).wait_recv()

    def a_sent():
        moved = a_buf.at[pl.ds(1, nd - 1)]
        remote(moved, moved, a_ss.at[0], a_rs.at[0], dev(s, flip(1), z)).wait_send()

    def og_copy(j):
        to = flip(j)
        src = og_ref.at[:, pl.ds(pl.multiple_of(to * cols, cols), cols)]
        return remote(src, og_buf.at[j], og_ss.at[0], og_rs.at[j - 1], dev(s, to, z))

    @pl.when(at_top)
    def _():
        a_start()

        ui_load.start()
        uii_load.start()

    q_load.start()
    signal_column(far_sem.at[0])
    w_load.wait()

    def in_features():
        tab_in[...] = sign_rows(seed_ref[0, 0], 0, width, scale)
        lifted = (x_ref[...].astype(F32) / rad_buf[:, :1] * gain_ref[...]).astype(BF16)
        return lax.dot_general(lifted, tab_in[...], NT, preferred_element_type=F32).astype(BF16)

    def pick_in(zt):
        entry = lax.broadcasted_iota(jnp.int32, (R, piece), 1) + zt * piece
        which = lax.broadcasted_iota(jnp.int32, (R, piece), 0)
        return (entry // R == which).astype(F32).astype(BF16)

    def pick_out():
        entry = lax.broadcasted_iota(jnp.int32, (R, piece), 1)
        which = lax.broadcasted_iota(jnp.int32, (R, piece), 0)
        return (entry % R == which).astype(F32).astype(BF16)

    def up_copy(c, first):
        src = p_buf.at[c] if first else uo_buf.at[c]
        return remote(src, un_buf.at[c], up_ss.at[0], up_rs.at[c], dev(s, d, jnp.minimum(z + 1, nz - 1)))

    def dn_copy(c, first):
        src = p_buf.at[c] if first else do_buf.at[c]
        return remote(src, dn_buf.at[c], dn_ss.at[0], dn_rs.at[c], dev(s, d, jnp.maximum(z - 1, 0)))

    def gn_copy(j, row, rows, h, to):
        return remote(
            gns_buf.at[j, pl.ds(row, rows)], gnr_buf.at[j, pl.ds(row, rows)],
            gn_ss.at[0], gn_rs.at[2 * j - 2 + h], dev(s, to, z),
        )

    def so_copy(j):
        return remote(so_buf.at[0, j], so_buf.at[1, j], so_ss.at[0], so_rs.at[j - 1], dev(0, flip(j), z))

    def slope_copy(j):
        src = so_buf.at[1, j] if j else so_buf.at[0, 0]
        return remote(src, slope_buf.at[z], sl_ss.at[0], sl_rs.at[0], dev(1, d, flip(j)))

    def slope_arrival():
        return remote(so_buf.at[0], slope_buf, sl_ss.at[0], sl_rs.at[0], dev(1 - s, d, z))

    def back(buf, j, row, rows):
        pre = gp_buf[j, pl.ds(row, rows)]
        both = jnp.dot(pre, wide_ref[...], preferred_element_type=F32)
        dot = dot_buf[j, pl.ds(row, rows)]
        high = dot.astype(BF16).astype(F32)
        lane = lax.broadcasted_iota(jnp.int32, (rows, lanes), 1)
        extra = jnp.where(lane == R, high, jnp.where(lane == R + 1, dot - high, both[:, feat:]))
        buf[j, pl.ds(row, rows), :feat] = both[:, :feat].astype(BF16)
        buf[j, pl.ds(row, rows), feat:] = extra.astype(BF16)

    def slope_of(total):
        sig = jax.nn.sigmoid(total)
        return sig * (1.0 + total * (1.0 - sig))

    lag_up = z * lag
    lag_dn = (nz - 1 - z) * lag
    lag_all = jnp.maximum(lag_up, lag_dn)
    slots = plane + gap + (nz - 1) * lag

    def chunk_at(v):
        valid = jnp.logical_and(v >= 0, v < plane + gap)
        valid = jnp.logical_and(valid, jnp.logical_or(v < nz, v >= nz + gap))
        return jnp.where(v < nz, v, v - gap), valid

    def relay(c, valid, gets, sends, copy, inbox, outbox):

        @pl.when(jnp.logical_and(valid, gets))
        def _():
            copy(c, True).wait_recv()

        @pl.when(jnp.logical_and(valid, jnp.logical_and(sends, jnp.logical_not(gets))))
        def _():
            copy(c, True).start()

        @pl.when(jnp.logical_and(valid, jnp.logical_and(sends, gets)))
        def _():
            outbox[c] = (inbox[c].astype(F32) + p_buf[c].astype(F32)).astype(BF16)
            copy(c, False).start()

    def sweep(on_block, on_total):
        def slot(i, carry):
            for j in range(nd):
                @pl.when(i == (j * nz + gap if j else 0))
                def _(j=j):
                    on_block(j)
                    multiply(j)

            c, valid = chunk_at(i - lag_up)
            relay(c, valid, z > 0, z < nz - 1, up_copy, un_buf, uo_buf)
            c, valid = chunk_at(i - lag_dn)
            relay(c, valid, z < nz - 1, z > 0, dn_copy, dn_buf, do_buf)
            c, valid = chunk_at(i - lag_all)
            q = lax.rem(jnp.maximum(c, 0), nz)
            j_now = lax.div(jnp.maximum(c, 0), nz)

            def total_of(up, dn):
                total = p_buf[c].astype(F32)
                if up:
                    total = total + un_buf[c].astype(F32)
                if dn:
                    total = total + dn_buf[c].astype(F32)
                on_total(j_now, q, total)

            @pl.when(jnp.logical_and(valid, z == 0))
            def _():
                total_of(False, True)

            @pl.when(jnp.logical_and(valid, z == nz - 1))
            def _():
                total_of(True, False)

            @pl.when(jnp.logical_and(valid, jnp.logical_and(z > 0, z < nz - 1)))
            def _():
                total_of(True, True)

            @pl.when(valid)
            def _():
                after_total(j_now, q)

            return carry

        lax.fori_loop(0, slots, slot, 0)

    def multiply(j):
        part = jnp.dot(a_buf[j], w_ref[...], preferred_element_type=F32).astype(BF16)
        for q in range(nz):
            p_buf[j * nz + q] = part[q * sub : (q + 1) * sub]

    def after_total(j, q):
        @pl.when(jnp.logical_and(q == nz - 1, j == 0))
        def _():
            back(gnr_buf, 0, 0, tok)

        for h in range(2):
            @pl.when(jnp.logical_and(q == (h + 1) * nz // 2 - 1, j > 0))
            def _(h=h):
                back(gns_buf, j, h * half, half)
                gn_copy(j, h * half, half, h, flip(j)).start()

    def sums_sent(ss, rs, count):
        moved = p_buf.at[pl.ds(0, count)]
        remote(moved, moved, ss.at[0], rs.at[0], dev(1 - s, d, z)).wait_send()

    def g_copy(o):
        return remote(g_buf.at[o % nz], gr_buf.at[mine], g_ss.at[0], g_rs.at[0], dev(0, o // nz, o % nz))

    def g1_copy(j):
        return remote(g1_buf, gr1_buf.at[j], g1_ss.at[0], g1_rs.at[0], dev(1, flip(j), z))

    def side_copy(which):
        src, dst = ((infs_buf, infr_buf), (tab_out, tabr_buf))[which]
        return remote(src, dst, side_ss.at[which], side_rs.at[which], dev(1, d, z))

    def side_arrival(which):
        src, dst = ((infs_buf, infr_buf), (tab_out, tabr_buf))[which]
        return remote(src, dst, side_ss.at[which], side_rs.at[which], dev(0, d, z))

    def sc_copy(o):
        to = lax.rem(here + o, column)
        return remote(
            sc_buf.at[here], sc_buf.at[here], sc_ss.at[0], sc_rs.at[0], dev(to // nz, d, lax.rem(to, nz))
        )

    def score():
        grads = out_ref[:, :piece]
        q_load.wait()
        queries = q_ref[...]
        high = grads.astype(BF16)
        rest = grads - high.astype(F32)
        middle = rest.astype(BF16)
        low = (rest - middle.astype(F32)).astype(BF16)
        part = lax.dot_general(high, queries, NT, preferred_element_type=F32)
        part = part + lax.dot_general(middle, queries, NT, preferred_element_type=F32)
        part = part + lax.dot_general(low, queries, NT, preferred_element_type=F32)
        sc_buf[here] = part
        for o in range(1, column):
            sc_copy(o).start()

    @pl.when(at_top)
    def _():
        def on_block(j):
            if j == 1:
                wide_ref[:, :feat] = w_ref[...].T
                wide_ref[:, feat:] = tab_out[...].T
            a_wait(j)
            if j == 1:
                signal(go_sem.at[0], dev(0, d, z))
            outer = jnp.logical_or(z == 0, z == nz - 1)

            @pl.when(outer if j == 2 else jnp.logical_and(j == 1, jnp.logical_not(outer)))
            def _():
                og_copy(1).start()
                og_copy(2).start()

            if j == 3:
                og_copy(3).start()

        def on_total(j, q, total):
            for each in range(nd):
                @pl.when(jnp.logical_and(q == 0, j == each))
                def _(each=each):
                    if each:
                        og_copy(each).wait_recv()
                    else:
                        ui_load.wait()

            rows = pl.ds(pl.multiple_of(q * sub, sub), sub)
            pre = (og_buf[j, rows].astype(F32) * slope_of(total)).astype(BF16)
            gp_buf[j, rows] = pre
            dot = jnp.sum(pre.astype(F32) * total, axis=1, keepdims=True)
            dot_buf[j, rows] = jnp.broadcast_to(dot, (sub, lanes))

        sweep(on_block, on_total)

        in_feat = in_features()
        g_left = jnp.dot(in_feat, pick_in(z), preferred_element_type=F32)
        left_buf[nz] = g_left
        for which in range(2):
            side_arrival(which).wait_recv()
        for zt in range(nz):
            left_buf[zt] = jnp.dot(infr_buf[:, :R], pick_in(zt), preferred_element_type=F32)
        uii_load.wait()
        pl.semaphore_wait(far_sem.at[0], column - 1)
        slope_arrival().wait_recv()
        for k in range(nz):
            if k * 2 % nz == 0:
                h = k * 2 // nz
                for j in range(1, nd):
                    gn_copy(j, h * half, half, h, d).wait_recv()
            rows = pl.ds(k * sub, sub)
            grad_norm = gnr_buf[0, rows, :feat].astype(F32)
            extra = gnr_buf[0, rows, feat:].astype(F32)
            for j in range(1, nd):
                grad_norm = grad_norm + gnr_buf[j, rows, :feat].astype(F32)
                extra = extra + gnr_buf[j, rows, feat:].astype(F32)
            dot_buf[0, rows] = extra
            mean_dot = (extra[:, R : R + 1] + extra[:, R + 1 : R + 2]) * (1.0 / width)
            scaled = grad_norm.astype(BF16).astype(F32) * gain_ref[:, pl.ds(z_start, feat)]
            change = (scaled - norm_buf[rows] * mean_dot) / rad_buf[rows, :1]
            upstream = (uii_buf[rows].astype(F32) + change).astype(BF16)
            low_buf[rows] = (upstream.astype(F32) * slope_buf[k].astype(F32)).astype(BF16)
        out_low = lax.dot_general(low_buf[...], tabr_buf[...], NT, preferred_element_type=F32)
        spread = pick_out()
        right = jnp.dot(out_low[:, :R].astype(BF16), spread, preferred_element_type=F32)
        for zt in range(nz):
            g_buf[zt] = jnp.sum(left_buf[zt] * right, axis=0, keepdims=True)
        for o in range(plane):
            g_copy(o).start()

        right = jnp.dot(dot_buf[0, :, :R].astype(BF16), spread, preferred_element_type=F32)
        own = jnp.sum(left_buf[nz] * right, axis=0, keepdims=True)
        g1_buf[...] = own
        for j in range(1, nd):
            g1_copy(j).start()
        gr1_buf[0] = own
        moved = gr1_buf.at[pl.ds(1, nd - 1)]
        remote(moved, moved, g1_ss.at[0], g1_rs.at[0], dev(0, d, z)).wait_recv()
        for k in range(SEQS):
            row = jnp.zeros((1, piece), F32)
            for group in range(SEQS):
                held = gr1_buf[group * per_seq]
                for j in range(group * per_seq + 1, (group + 1) * per_seq):
                    held = held + gr1_buf[j]
                row = row + jnp.where(lax.div(flip(group * per_seq), per_seq) == k, held, 0.0)
            out_ref[k : k + 1, :piece] = row
        score()
        moved = gns_buf.at[pl.ds(1, nd - 1)]
        remote(moved, moved, gn_ss.at[0], gn_rs.at[0], dev(0, d, z)).wait_send()
        moved = og_buf.at[pl.ds(1, nd - 1)]
        remote(moved, moved, og_ss.at[0], og_rs.at[0], dev(0, d, z)).wait_send()
        moved = gr1_buf.at[pl.ds(1, nd - 1)]
        remote(moved, moved, g1_ss.at[0], g1_rs.at[0], dev(0, d, z)).wait_send()
        remote(gr_buf, gr_buf, g_ss.at[0], g_rs.at[0], dev(0, d, z)).wait_send()
        a_sent()

        @pl.when(z < nz - 1)
        def _():
            sums_sent(up_ss, up_rs, plane)

        @pl.when(z > 0)
        def _():
            sums_sent(dn_ss, dn_rs, plane)


    @pl.when(jnp.logical_not(at_top))
    def _():
        low = z < nz // 2
        outer = jnp.logical_or(z == 0, z == nz - 1)
        inner_z = jnp.where(low, 1, nz - 2)
        outer_z = jnp.where(low, 0, nz - 1)

        def lift(src, c, to):
            return remote(src, un_buf.at[c], up_ss.at[0], up_rs.at[c], dev(0, d, to))

        def drop(src, c, to):
            return remote(src, dn_buf.at[c], dn_ss.at[0], dn_rs.at[c], dev(0, d, to))

        def hand_on(block):
            for o in range(1, nz):
                c = block * nz + jnp.where(low, nz - o, o - 1)

                @pl.when(jnp.logical_and(outer, low))
                def _(c=c):
                    lift(p_buf.at[c], c, inner_z).start()

                @pl.when(jnp.logical_and(outer, jnp.logical_not(low)))
                def _(c=c):
                    drop(p_buf.at[c], c, inner_z).start()

            c = block * nz + outer_z

            @pl.when(jnp.logical_and(jnp.logical_not(outer), low))
            def _():
                lift(p_buf.at[c], c, outer_z).start()

            @pl.when(jnp.logical_and(jnp.logical_not(outer), jnp.logical_not(low)))
            def _():
                drop(p_buf.at[c], c, outer_z).start()

        def pass_on(block):
            for o in range(nz // 2):
                to = jnp.where(low, nz - 1 - o, o)
                c = block * nz + to

                @pl.when(jnp.logical_and(jnp.logical_not(outer), low))
                def _(c=c, to=to):
                    lift(p_buf.at[c], c, to).wait_recv()
                    uo_buf[c] = (un_buf[c].astype(F32) + p_buf[c].astype(F32)).astype(BF16)
                    lift(uo_buf.at[c], c, to).start()

                @pl.when(jnp.logical_and(jnp.logical_not(outer), jnp.logical_not(low)))
                def _(c=c, to=to):
                    drop(p_buf.at[c], c, to).wait_recv()
                    uo_buf[c] = (dn_buf[c].astype(F32) + p_buf[c].astype(F32)).astype(BF16)
                    drop(uo_buf.at[c], c, to).start()

        def lower_slope(block):
            c = block * nz + z
            lift(p_buf.at[c], c, z).wait_recv()
            drop(p_buf.at[c], c, z).wait_recv()
            total = p_buf[c].astype(F32) + un_buf[c].astype(F32) + dn_buf[c].astype(F32)
            so_buf[0, block] = slope_of(total).astype(BF16)
            if block:
                so_copy(block).start()
            else:
                slope_copy(0).start()

        def forward(block):
            so_copy(block).wait_recv()
            slope_copy(block).start()

        multiply(0)
        hand_on(0)
        infs_buf[:, :R] = in_features()
        infs_buf[:, R:] = jnp.zeros((tok, lanes - R), BF16)
        for which in range(2):
            side_copy(which).start()
        pl.semaphore_wait(go_sem.at[0], 1)
        a_start()
        pl.semaphore_wait(far_sem.at[0], column - 1)
        pass_on(0)
        for block in range(1, nd):
            a_wait(block)
            multiply(block)
            hand_on(block)
            if block == 1:
                lower_slope(0)
        pass_on(1)
        for block in range(2, nd):
            pass_on(block)
            lower_slope(block - 1)
            if block > 2:
                forward(block - 2)
        lower_slope(nd - 1)
        for block in range(nd - 2, nd):
            forward(block)
        remote(gr_buf, gr_buf, g_ss.at[0], g_rs.at[0], dev(1, d, z)).wait_recv()
        for k in range(SEQS):
            held = gr_buf[k * per_seq * nz]
            for o in range(k * per_seq * nz + 1, (k + 1) * per_seq * nz):
                held = held + gr_buf[o]
            out_ref[k : k + 1, :piece] = held
        score()
        a_sent()
        moved = so_buf.at[0, pl.ds(1, nd - 1)]
        remote(moved, moved, so_ss.at[0], so_rs.at[0], dev(1, d, z)).wait_send()
        slope_arrival().wait_send()
        for which in range(2):
            side_copy(which).wait_send()
        @pl.when(low)
        def _():
            sums_sent(up_ss, up_rs, nd * (nz - 1))

        @pl.when(jnp.logical_not(low))
        def _():
            sums_sent(dn_ss, dn_rs, nd * (nz - 1))

    moved = sc_buf.at[pl.ds(0, column - 1)]
    others = remote(moved, moved, sc_ss.at[0], sc_rs.at[0], dev(1 - s, d, z))
    others.wait_recv()
    scores = sc_buf[0]
    for other in range(1, column):
        scores = scores + sc_buf[other]
    out_ref[:, piece : piece + scores.shape[1]] = scores
    others.wait_send()


def pair_call(nd, nz, tok, width, queries):
    feat, cols, sub, plane, column = width // nz, width // nd, tok // nz, nd * nz, 2 * nz
    piece, lanes = R * R // nz, 2 * R
    dma = pltpu.SemaphoreType.DMA
    sems = []
    for arrivals in (2 * nd - 2, nd - 1, plane, plane, 2 * nd - 2, nd - 1, 1):
        sems += [dma((1,)), dma((arrivals,))]
    sems += [dma((2,)), dma((2,))]
    for _ in range(3):
        sems += [dma((1,)), dma((1,))]
    vmem = pl.BlockSpec(memory_space=pltpu.VMEM)
    hbm = pl.BlockSpec(memory_space=pl.ANY)
    chunks = pltpu.VMEM((plane, sub, cols), BF16)
    blocks = pltpu.VMEM((nd, tok, cols), BF16)
    return pl.pallas_call(
        functools.partial(pair_kernel, nd, nz, LAG, GAP),
        out_shape=pltpu.VMEM((SEQS, piece + queries), F32),
        in_specs=[hbm, hbm, hbm, pl.BlockSpec(memory_space=pltpu.SMEM), hbm, hbm],
        out_specs=vmem,
        scratch_shapes=[
            pltpu.VMEM((tok, width), BF16),
            pltpu.VMEM((feat, cols), BF16),
            pltpu.VMEM((1, width), F32),
            pltpu.VMEM((queries, piece), BF16),
            pltpu.VMEM((cols, feat + lanes), BF16),
            pltpu.VMEM((R, width), BF16),
            pltpu.VMEM((lanes, cols), BF16),
            pltpu.VMEM((tok, feat), F32),
            pltpu.VMEM((tok, 128), F32),
            blocks, chunks, chunks, chunks, chunks, chunks,
            blocks,
            pltpu.VMEM((tok, feat), BF16),
            blocks,
            pltpu.VMEM((nd, tok, lanes), F32),
            pltpu.VMEM((nd, tok, feat + lanes), BF16),
            pltpu.VMEM((nd, tok, feat + lanes), BF16),
            pltpu.VMEM((2, nd, sub, cols), BF16),
            pltpu.VMEM((nz, sub, cols), BF16),
            pltpu.VMEM((lanes, cols), BF16),
            pltpu.VMEM((tok, lanes), BF16),
            pltpu.VMEM((tok, lanes), BF16),
            pltpu.VMEM((tok, cols), BF16),
            pltpu.VMEM((nz + 1, tok, piece), F32),
            pltpu.VMEM((nz, 1, piece), F32),
            pltpu.VMEM((plane, 1, piece), F32),
            pltpu.VMEM((1, piece), F32),
            pltpu.VMEM((nd, 1, piece), F32),
            pltpu.VMEM((column, SEQS, queries), F32),
            dma((6,)),
            pltpu.SemaphoreType.REGULAR((1,)),
            pltpu.SemaphoreType.REGULAR((1,)),
            *sems,
        ],
        compiler_params=pltpu.CompilerParams(
            collective_id=0, has_side_effects=True, vmem_limit_bytes=60 * 1024 * 1024
        ),
    )


def stack_call(sections, nd, nz, tok, width, queries):
    feat, cols = width // nz, width // nd
    sub = tok // nz
    piece = R * R // nz
    column = sections * nz
    plane = nd * nz
    vmem = pl.BlockSpec(memory_space=pltpu.VMEM)
    hbm = pl.BlockSpec(memory_space=pl.ANY)
    dma = pltpu.SemaphoreType.DMA
    sems = []
    for shape in ((nd,), (nd,), (nz, nd), (nd,), (nz, nd), (nd,), (plane,)):
        sems += [dma(shape), dma(shape)]
    sems += [dma((nz,)), dma((nd,)), dma((1,)), dma((1,))]
    sems += [dma((plane,)), dma((plane,)), dma((column,)), dma((column,))]
    return pl.pallas_call(
        functools.partial(kernel, sections, nd, nz),
        out_shape=jax.ShapeDtypeStruct((SEQS, piece + queries), F32),
        in_specs=[hbm, hbm, vmem, pl.BlockSpec(memory_space=pltpu.SMEM), hbm, vmem],
        out_specs=vmem,
        scratch_shapes=[
            pltpu.VMEM((nd, tok, feat), BF16),
            pltpu.VMEM((nd, sub, R), F32),
            pltpu.VMEM((nz, nd, sub, cols), BF16),
            pltpu.VMEM((nz, nd, sub, cols), BF16),
            pltpu.VMEM((nd, sub, cols), F32),
            pltpu.VMEM((nd, sub, cols), BF16),
            pltpu.VMEM((tok, feat), BF16),
            pltpu.VMEM((nz, nd, sub, cols), BF16),
            pltpu.VMEM((nd, tok, feat), BF16),
            pltpu.VMEM((nd, tok, feat), BF16),
            pltpu.VMEM((plane, 8, tok), F32),
            pltpu.VMEM((tok, feat), BF16),
            pltpu.VMEM((nz, SEQS, piece), F32),
            pltpu.VMEM((plane, SEQS, piece), F32),
            pltpu.VMEM((column, SEQS, queries), F32),
            pltpu.VMEM((tok, width), BF16),
            pltpu.VMEM((feat, cols), BF16),
            pltpu.VMEM((nd, sub, cols), F32),
            pltpu.VMEM((tok, feat), F32),
            pltpu.VMEM((tok, 128), F32),
            pltpu.VMEM((tok, tok), F32),
            pltpu.VMEM((nz, sub, tok), F32),
            pltpu.VMEM((nz, tok, piece), F32),
            pltpu.VMEM((nz, R, piece), BF16),
            *sems,
            dma((4,)),
            pltpu.SemaphoreType.REGULAR((2,)),
            pltpu.SemaphoreType.REGULAR((1,)),
        ],
        compiler_params=pltpu.CompilerParams(
            collective_id=0, has_side_effects=True, vmem_limit_bytes=60 * 1024 * 1024
        ),
    )


def part_outputs(both_ref, grads_ref, scores_ref):
    piece = grads_ref.shape[1]
    grads_ref[...] = both_ref[:, :piece]
    scores_ref[...] = both_ref[:, piece : piece + scores_ref.shape[1]]


def body(section_input, weights, gains, proj_seeds, out_grad, query_grads):
    sections = lax.axis_size("section")
    nd = lax.axis_size("dp")
    nz = lax.axis_size("tensor")
    tok, width = section_input.shape[1:]
    feat = weights.shape[1]
    cols = weights.shape[2]
    assert nd == nz and feat == cols
    piece = R * R // nz
    queries = query_grads.shape[1]
    vmem = pl.BlockSpec(memory_space=pltpu.VMEM)
    paired = sections == 2 and nd == 4 and nz == 4
    if paired:
        call = pair_call(nd, nz, tok, width, queries)
    else:
        call = stack_call(sections, nd, nz, tok, width, queries)
    out = call(section_input[0], weights[0], gains, proj_seeds, out_grad, query_grads[0])
    if paired:
        out = pltpu.with_memory_space_constraint(out, pltpu.VMEM)
    grads, scores = pl.pallas_call(
        part_outputs,
        out_shape=(
            jax.ShapeDtypeStruct((SEQS, piece), F32),
            jax.ShapeDtypeStruct((SEQS, queries), F32),
        ),
        in_specs=[vmem],
        out_specs=(vmem, vmem),
    )(out)
    return (grads[None], scores)


def solution(mesh):
    in_specs = (
        P("section", "dp", None),
        P("section", "tensor", "dp"),
        P("section", None),
        P("section", None),
        P("dp", None),
        P("section", "dp", "tensor"),
    )
    out_specs = (P("section", None, "tensor"), P(None, "dp"))
    return jax.shard_map(body, mesh=mesh, in_specs=in_specs, out_specs=out_specs, check_vma=False)
```

```python
import functools
import math

import jax
import jax.numpy as jnp
from jax import lax
from jax.experimental import pallas as pl
from jax.experimental.pallas import tpu as pltpu
from jax.sharding import PartitionSpec as P

R = 64
SEQS = 2
eps = 1e-05
F32 = jnp.float32
BF16 = jnp.bfloat16
MESH = pl.DeviceIdType.MESH
NT = (((1,), (1,)), ((), ()))
LAG = 6
GAP = 3
LOADS = 4


def sign_rows(seed_value, row_start, row_count, scale):
    row_index = lax.broadcasted_iota(jnp.int32, (R, row_count), 1) + row_start
    col_index = lax.broadcasted_iota(jnp.int32, (R, row_count), 0)
    mixing = row_index * 40503 + col_index * 9973 + (seed_value * 7919 + 12345)
    mixing = mixing ^ (mixing >> 13)
    mixing = mixing * 1274126177
    mixing = mixing ^ (mixing >> 16)
    parity = (mixing >> 10) & 1
    return jnp.where(parity == 1, scale, -scale).astype(BF16)


def kernel(
    sections, nd, nz,
    x_hbm, w_hbm, gain_ref, seed_ref, og_ref, q_ref,
    out_ref,
    a_buf, inf_buf, ps_buf, pr_buf, slope_buf, ui_buf, uii_buf, gp_buf,
    gns_buf, gnr_buf, dot_buf, up_buf, g_buf, gr_buf, sc_buf,
    x_ref, w_ref, sum_buf, norm_buf, rad_buf, turn_buf, mean_buf, left_buf, pick_buf,
    a_ss, a_rs, inf_ss, inf_rs, p_ss, p_rs, og_ss, og_rs, gp_ss, gp_rs,
    gn_ss, gn_rs, dt_ss, dt_rs, up_ss, up_rs, uii_ss, uii_rs,
    g_ss, g_rs, sc_ss, sc_rs, in_sem, go_sem, far_sem,
):
    s = lax.axis_index("section")
    d = lax.axis_index("dp")
    z = lax.axis_index("tensor")
    tok, width = x_hbm.shape
    feat = width // nz
    cols = width // nd
    sub = tok // nz
    at_top = s == sections - 1
    below_top = s == sections - 2
    lower = s > 0
    z_start = pl.multiple_of(z * feat, feat)
    d_start = pl.multiple_of(d * cols, cols)
    sub_start = pl.multiple_of(z * sub, sub)
    sub_start_d = pl.multiple_of(d * sub, sub)

    def dev(s_to, d_to, z_to):
        return {"section": s_to, "dp": d_to, "tensor": z_to}

    def remote(src, dst, ss, rs, to):
        return pltpu.make_async_remote_copy(
            src_ref=src, dst_ref=dst, send_sem=ss, recv_sem=rs, device_id=to, device_id_type=MESH
        )

    x_load = pltpu.make_async_copy(x_hbm, x_ref, in_sem.at[0])
    w_load = pltpu.make_async_copy(w_hbm, w_ref, in_sem.at[1])
    x_load.start()
    w_load.start()

    barrier = pltpu.get_barrier_semaphore()
    column = sections * nz
    here = s * nz + z

    def signal_column(sem):
        for o in range(1, column):
            to = lax.rem(here + o, column)
            pl.semaphore_signal(
                sem, inc=1, device_id=dev(to // nz, d, lax.rem(to, nz)), device_id_type=MESH
            )

    for o in range(1, nd):
        pl.semaphore_signal(
            barrier, inc=1, device_id=dev(s, lax.rem(d + o, nd), z), device_id_type=MESH
        )
    signal_column(barrier)

    x_load.wait()
    hidden = x_ref[...].astype(F32)
    radius = jnp.sqrt(jnp.mean(hidden * hidden, axis=1, keepdims=True) + eps)
    gain_z = gain_ref[:, pl.ds(z_start, feat)]
    normed_z = x_ref[:, pl.ds(z_start, feat)].astype(F32) / radius
    norm_buf[...] = normed_z
    rad_buf[...] = jnp.broadcast_to(radius, rad_buf.shape)
    a_buf[d] = (normed_z * gain_z).astype(BF16)

    pl.semaphore_wait(barrier, nd - 1 + column - 1)

    def a_copy(o):
        to = lax.rem(d + o, nd)
        return remote(a_buf.at[d], a_buf.at[d], a_ss.at[o], a_rs.at[o], dev(s, to, z))

    @pl.when(jnp.logical_not(below_top))
    def _():
        for o in range(1, nd):
            a_copy(o).start()

    def og_copy(o):
        to = lax.rem(d + o, nd)
        src = og_ref.at[pl.ds(sub_start, sub), pl.ds(pl.multiple_of(to * cols, cols), cols)]
        return remote(src, ui_buf.at[d], og_ss.at[o], og_rs.at[o], dev(s, to, z))

    def ui_load():
        src = og_ref.at[pl.ds(sub_start, sub), pl.ds(d_start, cols)]
        return pltpu.make_async_copy(src, ui_buf.at[d], in_sem.at[2])

    def uii_load():
        return pltpu.make_async_copy(og_ref.at[:, pl.ds(z_start, feat)], uii_buf, in_sem.at[3])

    @pl.when(at_top)
    def _():
        for o in range(1, nd):
            og_copy(o).start()
        ui_load().start()
        uii_load().start()

    @pl.when(below_top)
    def _():
        pl.semaphore_wait(go_sem.at[0], 1)
        for o in range(1, nd):
            a_copy(o).start()

    signal_column(far_sem.at[0])

    w_load.wait()

    def p_copy(o, block):
        to = lax.rem(z + o, nz)
        return remote(
            ps_buf.at[to, block], pr_buf.at[z, block], p_ss.at[o, block], p_rs.at[o, block],
            dev(s, d, to),
        )

    for o in range(nd):
        block = lax.rem(d + nd - o, nd)
        if o:
            a_copy(o).wait_recv()
        part = jnp.dot(a_buf[block], w_ref[...], preferred_element_type=F32).astype(BF16)
        for zt in range(nz):
            ps_buf[zt, block] = part[zt * sub : (zt + 1) * sub, :]

        @pl.when(jnp.logical_not(below_top))
        def _():
            for oz in range(1, nz):
                p_copy(oz, block).start()

    for o in range(1, nd):
        a_copy(o).wait_send()

    def go(which):
        pl.semaphore_signal(
            go_sem.at[which], inc=1, device_id=dev(jnp.maximum(s - 1, 0), d, z), device_id_type=MESH
        )

    if sections > 1:
        @pl.when(at_top)
        def _():
            go(0)

    scale = 1.0 / math.sqrt(width)
    x_sub = x_ref[pl.ds(sub_start, sub), :].astype(F32)
    radius_sub = jnp.sqrt(jnp.mean(x_sub * x_sub, axis=1, keepdims=True) + eps)
    lifted_sub = (x_sub / radius_sub * gain_ref[...]).astype(BF16)
    table_in = sign_rows(seed_ref[0, 0], 0, width, scale)
    inf_buf[d] = lax.dot_general(lifted_sub, table_in, NT, preferred_element_type=F32)

    def inf_copy(o):
        to = lax.rem(d + o, nd)
        return remote(inf_buf.at[d], inf_buf.at[d], inf_ss.at[o], inf_rs.at[o], dev(s, to, z))

    for o in range(1, nd):
        inf_copy(o).start()


    piece = R * R // nz
    per_seq = nd * sub // SEQS

    def spread():
        for o in range(1, nd):
            inf_copy(o).wait_recv()
        in_feat = inf_buf[...].reshape(nd * sub, R).astype(BF16)
        for zt in range(nz):
            entry = lax.broadcasted_iota(jnp.int32, (R, piece), 1) + zt * piece
            which = lax.broadcasted_iota(jnp.int32, (R, piece), 0)
            pick_in = (entry // R == which).astype(F32).astype(BF16)
            pick_buf[zt] = (entry % R == which).astype(F32).astype(BF16)
            left_buf[zt] = jnp.dot(in_feat, pick_in, preferred_element_type=F32)

    @pl.when(jnp.logical_not(at_top))
    def _():
        spread()

    if sections > 1:
        @pl.when(below_top)
        def _():
            pl.semaphore_wait(go_sem.at[1], 1)
            for o in range(nd):
                block = lax.rem(d + nd - o, nd)
                for oz in range(1, nz):
                    p_copy(oz, block).start()

    table_out = sign_rows(seed_ref[0, 1], d_start, cols, scale)

    def gp_copy(o, block):
        to = lax.rem(z + o, nz)
        return remote(
            gp_buf.at[z, block], gp_buf.at[z, block], gp_ss.at[o, block], gp_rs.at[o, block],
            dev(s, d, to),
        )

    for o in range(nd):
        block = lax.rem(d + nd - o, nd)
        summed = ps_buf[z, block].astype(F32)
        for oz in range(1, nz):
            p_copy(oz, block).wait_recv()
            summed = summed + pr_buf[lax.rem(z + nz - oz, nz), block].astype(F32)
        sig = jax.nn.sigmoid(summed)
        slope = sig * (1.0 + summed * (1.0 - sig))
        sum_buf[block] = summed
        slope_buf[block] = slope

        @pl.when(at_top)
        def _():
            if o:
                og_copy(o).wait_recv()
            else:
                ui_load().wait()
            gp_buf[z, block] = (ui_buf[block].astype(F32) * slope).astype(BF16)
            if sections > 1:
                for oz in range(1, nz):
                    gp_copy(oz, block).start()

    def up_copy(zt, source):
        return remote(
            up_buf.at[pl.ds(zt * sub, sub)], ui_buf.at[source], up_ss.at[zt], up_rs.at[source],
            dev(jnp.maximum(s - 1, 0), z, zt),
        )

    def uii_copy():
        return remote(up_buf, uii_buf, uii_ss.at[0], uii_rs.at[0], dev(jnp.maximum(s - 1, 0), d, z))

    @pl.when(at_top)
    def _():
        uii_load().wait()
        spread()

    @pl.when(jnp.logical_not(at_top))
    def _():
        for source in range(nd):
            up_copy(0, source).wait_recv()
        gp_buf[z] = (ui_buf[...].astype(F32) * slope_buf[...]).astype(BF16)

        @pl.when(lower)
        def _():
            for block in range(nd):
                for oz in range(1, nz):
                    gp_copy(oz, block).start()

    pl.semaphore_wait(far_sem.at[0], column - 1)
    grad_pre = gp_buf[z]
    plane = nd * nz
    mine = d * nz + z

    def dt_copy(o):
        to = lax.rem(mine + o, plane)
        return remote(
            dot_buf.at[mine], dot_buf.at[mine], dt_ss.at[o], dt_rs.at[o],
            dev(s, to // nz, lax.rem(to, nz)),
        )

    @pl.when(lower)
    def _():
        pre = gp_buf[z].astype(F32) * sum_buf[...]
        own_dot = jnp.sum(pre.reshape(nd * sub, cols), axis=1, keepdims=True)
        dot_buf[mine] = jnp.broadcast_to(own_dot, (tok, tok)).T[:8, :]
        for o in range(1, plane):
            dt_copy(o).start()

    out_feat = lax.dot_general(
        grad_pre.reshape(nd * sub, cols), table_out, NT, preferred_element_type=F32
    ).astype(BF16)
    for zt in range(nz):
        product = left_buf[zt] * jnp.dot(out_feat, pick_buf[zt], preferred_element_type=F32)
        for k in range(SEQS):
            g_buf[zt, k : k + 1, :] = jnp.sum(
                product[k * per_seq : (k + 1) * per_seq], axis=0, keepdims=True
            )

    def g_copy(o):
        to = lax.rem(mine + o, plane)
        return remote(
            g_buf.at[lax.rem(to, nz)], gr_buf.at[mine], g_ss.at[o], g_rs.at[o],
            dev(s, to // nz, lax.rem(to, nz)),
        )

    for o in range(1, plane):
        g_copy(o).start()
    gr_buf[mine] = g_buf[z]

    def gn_copy(o):
        to = lax.rem(d + nd - o, nd)
        return remote(gns_buf.at[to], gnr_buf.at[d], gn_ss.at[o], gn_rs.at[o], dev(s, to, z))

    @pl.when(lower)
    def _():
        for o in range(nd):
            block = lax.rem(d + nd - o, nd)
            for oz in range(1, nz):
                gp_copy(oz, block).wait_recv()
            if o == nd - 1:
                for each in range(nd):
                    for oz in range(1, nz):
                        gp_copy(oz, each).wait_send()

                @pl.when(at_top)
                def _():
                    go(1)

            rows = gp_buf[:, block].reshape(tok, cols)
            part = lax.dot_general(rows, w_ref[...], NT, preferred_element_type=F32).astype(BF16)
            if o:
                gns_buf[block] = part
                gn_copy(o).start()
            else:
                gnr_buf[d] = part
        for o in range(1, plane):
            dt_copy(o).wait_recv()
        for zt in range(nz):
            dots = dot_buf[zt]
            for dt in range(1, nd):
                dots = dots + dot_buf[dt * nz + zt]
            turn_buf[...] = jnp.broadcast_to(dots[:1, :] * (1.0 / width), (tok, tok)).T
            mean_buf[zt] = turn_buf[pl.ds(sub_start_d, sub), :]
        for o in range(1, nd):
            gn_copy(o).wait_recv()
        if sections > 2:
            @pl.when(jnp.logical_not(at_top))
            def _():
                uii_copy().wait_recv()
        for zt in range(nz):
            rows = pl.ds(zt * sub, sub)
            grad_norm = gnr_buf[0, rows].astype(F32)
            for dt in range(1, nd):
                grad_norm = grad_norm + gnr_buf[dt, rows].astype(F32)
            scaled = grad_norm.astype(BF16).astype(F32) * gain_ref[:, pl.ds(z_start, feat)]
            change = (scaled - norm_buf[rows] * mean_buf[zt][:, :1]) / rad_buf[rows, :1]
            up_buf[rows] = (uii_buf[rows].astype(F32) + change).astype(BF16)
            up_copy(zt, d).start()
        if sections > 2:
            @pl.when(s > 1)
            def _():
                uii_copy().start()

    for o in range(1, plane):
        g_copy(o).wait_recv()
    grads = gr_buf[0]
    for other in range(1, plane):
        grads = grads + gr_buf[other]
    out_ref[:, :piece] = grads
    queries = q_ref[...]
    high = grads.astype(BF16)
    rest = grads - high.astype(F32)
    middle = rest.astype(BF16)
    low = (rest - middle.astype(F32)).astype(BF16)
    part = lax.dot_general(high, queries, NT, preferred_element_type=F32)
    part = part + lax.dot_general(middle, queries, NT, preferred_element_type=F32)
    part = part + lax.dot_general(low, queries, NT, preferred_element_type=F32)
    sc_buf[here] = part

    def sc_copy(o):
        to = lax.rem(here + o, column)
        return remote(
            sc_buf.at[here], sc_buf.at[here], sc_ss.at[o], sc_rs.at[o],
            dev(to // nz, d, lax.rem(to, nz)),
        )

    for o in range(1, column):
        sc_copy(o).start()

    for o in range(1, nd):
        inf_copy(o).wait_send()
    for block in range(nd):
        for oz in range(1, nz):
            p_copy(oz, block).wait_send()

    @pl.when(at_top)
    def _():
        for o in range(1, nd):
            og_copy(o).wait_send()

    @pl.when(lower)
    def _():
        for o in range(1, plane):
            dt_copy(o).wait_send()
        for o in range(1, nd):
            gn_copy(o).wait_send()
        for zt in range(nz):
            up_copy(zt, d).wait_send()
        if sections > 2:
            @pl.when(s > 1)
            def _():
                uii_copy().wait_send()

    for o in range(1, plane):
        g_copy(o).wait_send()
    for o in range(1, column):
        sc_copy(o).wait_recv()
    scores = sc_buf[0]
    for other in range(1, column):
        scores = scores + sc_buf[other]
    out_ref[:, piece : piece + scores.shape[1]] = scores
    for o in range(1, column):
        sc_copy(o).wait_send()


def pair_kernel(
    nd, nz, lag, gap,
    x_hbm, w_hbm, gain_hbm, seed_ref, og_ref, q_hbm,
    out_ref,
    x_ref, w_ref, gain_ref, q_ref, wide_ref, tab_in, tab_out, norm_buf, rad_buf,
    a_buf, p_buf, un_buf, uo_buf, dn_buf, do_buf,
    og_buf, uii_buf, gp_buf, dot_buf, gns_buf, gnr_buf,
    so_buf, slope_buf, tabr_buf, infs_buf, infr_buf, low_buf,
    left_buf, g_buf, gr_buf, g1_buf, gr1_buf, sc_buf, stack_buf,
    in_sem, go_sem, far_sem,
    a_ss, a_rs, og_ss, og_rs, up_ss, up_rs, dn_ss, dn_rs, gn_ss, gn_rs,
    so_ss, so_rs, sl_ss, sl_rs, side_ss, side_rs, g_ss, g_rs, g1_ss, g1_rs, sc_ss, sc_rs,
):
    s = lax.axis_index("section")
    d = lax.axis_index("dp")
    z = lax.axis_index("tensor")
    tok, width = x_hbm.shape
    feat = width // nz
    cols = width // nd
    sub = tok // nz
    plane = nd * nz
    column = 2 * nz
    piece = R * R // nz
    lanes = tab_out.shape[0]
    half = tok // 2
    per_seq = nd // SEQS
    at_top = s == 1
    z_start = pl.multiple_of(z * feat, feat)
    d_start = pl.multiple_of(d * cols, cols)
    here = s * nz + z
    mine = d * nz + z
    scale = 1.0 / math.sqrt(width)

    def dev(s_to, d_to, z_to):
        return {"section": s_to, "dp": d_to, "tensor": z_to}

    def flip(j):
        to, bit = d, 1
        while bit < nd:
            flag = (j // bit) % 2 if isinstance(j, int) else lax.rem(lax.div(j, bit), 2)
            to = to + flag * bit * (1 - 2 * lax.rem(lax.div(d, bit), 2))
            bit *= 2
        return to

    def remote(src, dst, ss, rs, to):
        return pltpu.make_async_remote_copy(
            src_ref=src, dst_ref=dst, send_sem=ss, recv_sem=rs, device_id=to, device_id_type=MESH
        )

    def signal(sem, to):
        pl.semaphore_signal(sem, inc=1, device_id=to, device_id_type=MESH)

    x_load = pltpu.make_async_copy(x_hbm, x_ref, in_sem.at[0])
    w_load = pltpu.make_async_copy(w_hbm, w_ref, in_sem.at[1])

    def load(hbm, ref, sem, parts):
        rows = hbm.shape[0] // parts
        for part in range(parts):
            span = pl.ds(part * rows, rows)
            pltpu.make_async_copy(hbm.at[span], ref.at[span], sem).start()

    gain_load = pltpu.make_async_copy(gain_hbm, gain_ref, in_sem.at[4])
    q_load = pltpu.make_async_copy(q_hbm, q_ref, in_sem.at[5])
    load(x_hbm, x_ref, in_sem.at[0], LOADS)
    gain_load.start()
    load(w_hbm, w_ref, in_sem.at[1], LOADS)
    barrier = pltpu.get_barrier_semaphore()

    def signal_column(sem):
        for o in range(1, column):
            to = lax.rem(here + o, column)
            signal(sem, dev(to // nz, d, lax.rem(to, nz)))

    for j in range(1, nd):
        signal(barrier, dev(s, flip(j), z))
    signal_column(barrier)

    ui_load = pltpu.make_async_copy(og_ref.at[:, pl.ds(d_start, cols)], og_buf.at[0], in_sem.at[2])
    uii_load = pltpu.make_async_copy(og_ref.at[:, pl.ds(z_start, feat)], uii_buf, in_sem.at[3])

    table_row = jnp.where(at_top, d_start, z_start)
    tab_out[:R] = sign_rows(seed_ref[0, 1], table_row, cols, scale)
    tab_out[R:] = jnp.zeros((lanes - R, cols), BF16)
    x_load.wait()
    gain_load.wait()
    hidden = x_ref[...].astype(F32)
    radius = jnp.sqrt(jnp.mean(hidden * hidden, axis=1, keepdims=True) + eps)
    normed_z = x_ref[:, pl.ds(z_start, feat)].astype(F32) / radius
    norm_buf[...] = normed_z
    rad_buf[...] = jnp.broadcast_to(radius, rad_buf.shape)
    a_buf[0] = (normed_z * gain_ref[:, pl.ds(z_start, feat)]).astype(BF16)

    pl.semaphore_wait(barrier, nd - 1 + column - 1)

    def a_copy(j, h, via=0):
        rows = pl.ds(h * half, half)
        return remote(
            a_buf.at[via, rows], a_buf.at[j, rows], a_ss.at[0], a_rs.at[2 * j + h - 2],
            dev(s, flip(j - via), z),
        )

    def a_start():
        a_copy(1, 0).start()
        a_copy(2, 1).start()
        a_copy(1, 1).start()
        a_copy(2, 0).start()

    def a_wait(j):
        if j == 1:
            a_copy(1, 0).wait_recv()
            a_copy(3, 0, 1).start()
            a_copy(2, 1).wait_recv()
            a_copy(3, 1, 2).start()
            a_copy(1, 1).wait_recv()
        if j == 2:
            a_copy(2, 0).wait_recv()
        if j == 3:
            for h in range(2):
                a_copy(3, h).wait_recv()

    def a_sent():
        moved = a_buf.at[pl.ds(1, nd - 1)]
        remote(moved, moved, a_ss.at[0], a_rs.at[0], dev(s, flip(1), z)).wait_send()

    def og_copy(j):
        to = flip(j)
        src = og_ref.at[:, pl.ds(pl.multiple_of(to * cols, cols), cols)]
        return remote(src, og_buf.at[j], og_ss.at[0], og_rs.at[j - 1], dev(s, to, z))

    @pl.when(at_top)
    def _():
        a_start()

        ui_load.start()
        uii_load.start()

    q_load.start()
    signal_column(far_sem.at[0])
    w_load.wait()

    def in_features():
        tab_in[...] = sign_rows(seed_ref[0, 0], 0, width, scale)
        lifted = (x_ref[...].astype(F32) / rad_buf[:, :1] * gain_ref[...]).astype(BF16)
        return lax.dot_general(lifted, tab_in[...], NT, preferred_element_type=F32).astype(BF16)

    def pick_in(zt):
        entry = lax.broadcasted_iota(jnp.int32, (R, piece), 1) + zt * piece
        which = lax.broadcasted_iota(jnp.int32, (R, piece), 0)
        return (entry // R == which).astype(F32).astype(BF16)

    def pick_out():
        entry = lax.broadcasted_iota(jnp.int32, (R, piece), 1)
        which = lax.broadcasted_iota(jnp.int32, (R, piece), 0)
        return (entry % R == which).astype(F32).astype(BF16)

    def up_copy(c, first):
        src = p_buf.at[c] if first else uo_buf.at[c]
        return remote(src, un_buf.at[c], up_ss.at[0], up_rs.at[c], dev(s, d, jnp.minimum(z + 1, nz - 1)))

    def dn_copy(c, first):
        src = p_buf.at[c] if first else do_buf.at[c]
        return remote(src, dn_buf.at[c], dn_ss.at[0], dn_rs.at[c], dev(s, d, jnp.maximum(z - 1, 0)))

    def gn_copy(j, row, rows, h, to):
        return remote(
            gns_buf.at[j, pl.ds(row, rows)], gnr_buf.at[j, pl.ds(row, rows)],
            gn_ss.at[0], gn_rs.at[2 * j - 2 + h], dev(s, to, z),
        )

    def so_copy(j):
        return remote(so_buf.at[0, j], so_buf.at[1, j], so_ss.at[0], so_rs.at[j - 1], dev(0, flip(j), z))

    def slope_copy(j):
        src = so_buf.at[1, j] if j else so_buf.at[0, 0]
        return remote(src, slope_buf.at[z], sl_ss.at[0], sl_rs.at[0], dev(1, d, flip(j)))

    def slope_arrival():
        return remote(so_buf.at[0], slope_buf, sl_ss.at[0], sl_rs.at[0], dev(1 - s, d, z))

    def back(buf, j, row, rows):
        pre = gp_buf[j, pl.ds(row, rows)]
        both = jnp.dot(pre, wide_ref[...], preferred_element_type=F32)
        dot = dot_buf[j, pl.ds(row, rows)]
        high = dot.astype(BF16).astype(F32)
        lane = lax.broadcasted_iota(jnp.int32, (rows, lanes), 1)
        extra = jnp.where(lane == R, high, jnp.where(lane == R + 1, dot - high, both[:, feat:]))
        buf[j, pl.ds(row, rows), :feat] = both[:, :feat].astype(BF16)
        buf[j, pl.ds(row, rows), feat:] = extra.astype(BF16)

    def slope_of(total):
        sig = jax.nn.sigmoid(total)
        return sig * (1.0 + total * (1.0 - sig))

    lag_up = z * lag
    lag_dn = (nz - 1 - z) * lag
    lag_all = jnp.maximum(lag_up, lag_dn)
    slots = plane + gap + (nz - 1) * lag

    def chunk_at(v):
        valid = jnp.logical_and(v >= 0, v < plane + gap)
        valid = jnp.logical_and(valid, jnp.logical_or(v < nz, v >= nz + gap))
        return jnp.where(v < nz, v, v - gap), valid

    def relay(c, valid, gets, sends, copy, inbox, outbox):

        @pl.when(jnp.logical_and(valid, gets))
        def _():
            copy(c, True).wait_recv()

        @pl.when(jnp.logical_and(valid, jnp.logical_and(sends, jnp.logical_not(gets))))
        def _():
            copy(c, True).start()

        @pl.when(jnp.logical_and(valid, jnp.logical_and(sends, gets)))
        def _():
            outbox[c] = (inbox[c].astype(F32) + p_buf[c].astype(F32)).astype(BF16)
            copy(c, False).start()

    def sweep(on_block, on_total):
        def slot(i, carry):
            for j in range(nd):
                @pl.when(i == (j * nz + gap if j else 0))
                def _(j=j):
                    on_block(j)
                    multiply(j)

            c, valid = chunk_at(i - lag_up)
            relay(c, valid, z > 0, z < nz - 1, up_copy, un_buf, uo_buf)
            c, valid = chunk_at(i - lag_dn)
            relay(c, valid, z < nz - 1, z > 0, dn_copy, dn_buf, do_buf)
            c, valid = chunk_at(i - lag_all)
            q = lax.rem(jnp.maximum(c, 0), nz)
            j_now = lax.div(jnp.maximum(c, 0), nz)

            def total_of(up, dn):
                total = p_buf[c].astype(F32)
                if up:
                    total = total + un_buf[c].astype(F32)
                if dn:
                    total = total + dn_buf[c].astype(F32)
                on_total(j_now, q, total)

            @pl.when(jnp.logical_and(valid, z == 0))
            def _():
                total_of(False, True)

            @pl.when(jnp.logical_and(valid, z == nz - 1))
            def _():
                total_of(True, False)

            @pl.when(jnp.logical_and(valid, jnp.logical_and(z > 0, z < nz - 1)))
            def _():
                total_of(True, True)

            @pl.when(valid)
            def _():
                after_total(j_now, q)

            return carry

        lax.fori_loop(0, slots, slot, 0)

    def multiply(j):
        part = jnp.dot(a_buf[j], w_ref[...], preferred_element_type=F32).astype(BF16)
        for q in range(nz):
            p_buf[j * nz + q] = part[q * sub : (q + 1) * sub]

    def after_total(j, q):
        @pl.when(jnp.logical_and(q == nz - 1, j == 0))
        def _():
            back(gnr_buf, 0, 0, tok)

        for h in range(2):
            @pl.when(jnp.logical_and(q == (h + 1) * nz // 2 - 1, j > 0))
            def _(h=h):
                back(gns_buf, j, h * half, half)
                gn_copy(j, h * half, half, h, flip(j)).start()

    def sums_sent(ss, rs, count):
        moved = p_buf.at[pl.ds(0, count)]
        remote(moved, moved, ss.at[0], rs.at[0], dev(1 - s, d, z)).wait_send()

    def g_copy(o):
        return remote(g_buf.at[o % nz], gr_buf.at[mine], g_ss.at[0], g_rs.at[0], dev(0, o // nz, o % nz))

    def g1_copy(j):
        return remote(g1_buf, gr1_buf.at[j], g1_ss.at[0], g1_rs.at[0], dev(1, flip(j), z))

    def side_copy(which):
        src, dst = ((infs_buf, infr_buf), (tab_out, tabr_buf))[which]
        return remote(src, dst, side_ss.at[which], side_rs.at[which], dev(1, d, z))

    def side_arrival(which):
        src, dst = ((infs_buf, infr_buf), (tab_out, tabr_buf))[which]
        return remote(src, dst, side_ss.at[which], side_rs.at[which], dev(0, d, z))

    def sc_copy(o):
        to = lax.rem(here + o, column)
        return remote(
            sc_buf.at[here], sc_buf.at[here], sc_ss.at[0], sc_rs.at[0], dev(to // nz, d, lax.rem(to, nz))
        )

    def score():
        grads = out_ref[:, :piece]
        q_load.wait()
        queries = q_ref[...]
        high = grads.astype(BF16).astype(F32)
        middle = (grads - high).astype(BF16).astype(F32)
        stack_buf[:SEQS] = high
        stack_buf[SEQS : 2 * SEQS] = middle
        stack_buf[2 * SEQS : 3 * SEQS] = grads - high - middle
        parts = lax.dot_general(stack_buf[...].astype(BF16), queries, NT, preferred_element_type=F32)
        part = parts[:SEQS] + parts[SEQS : 2 * SEQS] + parts[2 * SEQS : 3 * SEQS]
        sc_buf[here] = part
        for o in range(1, column):
            sc_copy(o).start()

    @pl.when(at_top)
    def _():
        def on_block(j):
            if j == 1:
                wide_ref[:, :feat] = w_ref[...].T
                wide_ref[:, feat:] = tab_out[...].T
            a_wait(j)
            if j == 1:
                signal(go_sem.at[0], dev(0, d, z))
            outer = jnp.logical_or(z == 0, z == nz - 1)

            @pl.when(outer if j == 2 else jnp.logical_and(j == 1, jnp.logical_not(outer)))
            def _():
                og_copy(1).start()
                og_copy(2).start()

            if j == 3:
                og_copy(3).start()

        def on_total(j, q, total):
            for each in range(nd):
                @pl.when(jnp.logical_and(q == 0, j == each))
                def _(each=each):
                    if each:
                        og_copy(each).wait_recv()
                    else:
                        ui_load.wait()

            rows = pl.ds(pl.multiple_of(q * sub, sub), sub)
            pre = (og_buf[j, rows].astype(F32) * slope_of(total)).astype(BF16)
            gp_buf[j, rows] = pre
            dot = jnp.sum(pre.astype(F32) * total, axis=1, keepdims=True)
            dot_buf[j, rows] = jnp.broadcast_to(dot, (sub, lanes))

        sweep(on_block, on_total)

        in_feat = in_features()
        g_left = jnp.dot(in_feat, pick_in(z), preferred_element_type=F32)
        left_buf[nz] = g_left
        for which in range(2):
            side_arrival(which).wait_recv()
        for zt in range(nz):
            left_buf[zt] = jnp.dot(infr_buf[:, :R], pick_in(zt), preferred_element_type=F32)
        uii_load.wait()
        pl.semaphore_wait(far_sem.at[0], column - 1)
        slope_arrival().wait_recv()
        for k in range(nz):
            if k * 2 % nz == 0:
                h = k * 2 // nz
                for j in range(1, nd):
                    gn_copy(j, h * half, half, h, d).wait_recv()
            rows = pl.ds(k * sub, sub)
            grad_norm = gnr_buf[0, rows, :feat].astype(F32)
            extra = gnr_buf[0, rows, feat:].astype(F32)
            for j in range(1, nd):
                grad_norm = grad_norm + gnr_buf[j, rows, :feat].astype(F32)
                extra = extra + gnr_buf[j, rows, feat:].astype(F32)
            dot_buf[0, rows] = extra
            mean_dot = (extra[:, R : R + 1] + extra[:, R + 1 : R + 2]) * (1.0 / width)
            scaled = grad_norm.astype(BF16).astype(F32) * gain_ref[:, pl.ds(z_start, feat)]
            change = (scaled - norm_buf[rows] * mean_dot) / rad_buf[rows, :1]
            upstream = (uii_buf[rows].astype(F32) + change).astype(BF16)
            low_buf[rows] = (upstream.astype(F32) * slope_buf[k].astype(F32)).astype(BF16)
        out_low = lax.dot_general(low_buf[...], tabr_buf[...], NT, preferred_element_type=F32)
        spread = pick_out()
        right = jnp.dot(out_low[:, :R].astype(BF16), spread, preferred_element_type=F32)
        for zt in range(nz):
            g_buf[zt] = jnp.sum(left_buf[zt] * right, axis=0, keepdims=True)
        for o in range(plane):
            g_copy(o).start()

        right = jnp.dot(dot_buf[0, :, :R].astype(BF16), spread, preferred_element_type=F32)
        own = jnp.sum(left_buf[nz] * right, axis=0, keepdims=True)
        g1_buf[...] = own
        for j in range(1, nd):
            g1_copy(j).start()
        gr1_buf[0] = own
        moved = gr1_buf.at[pl.ds(1, nd - 1)]
        remote(moved, moved, g1_ss.at[0], g1_rs.at[0], dev(0, d, z)).wait_recv()
        for k in range(SEQS):
            row = jnp.zeros((1, piece), F32)
            for group in range(SEQS):
                held = gr1_buf[group * per_seq]
                for j in range(group * per_seq + 1, (group + 1) * per_seq):
                    held = held + gr1_buf[j]
                row = row + jnp.where(lax.div(flip(group * per_seq), per_seq) == k, held, 0.0)
            out_ref[k : k + 1, :piece] = row
        score()
        moved = gns_buf.at[pl.ds(1, nd - 1)]
        remote(moved, moved, gn_ss.at[0], gn_rs.at[0], dev(0, d, z)).wait_send()
        moved = og_buf.at[pl.ds(1, nd - 1)]
        remote(moved, moved, og_ss.at[0], og_rs.at[0], dev(0, d, z)).wait_send()
        moved = gr1_buf.at[pl.ds(1, nd - 1)]
        remote(moved, moved, g1_ss.at[0], g1_rs.at[0], dev(0, d, z)).wait_send()
        remote(gr_buf, gr_buf, g_ss.at[0], g_rs.at[0], dev(0, d, z)).wait_send()
        a_sent()

        @pl.when(z < nz - 1)
        def _():
            sums_sent(up_ss, up_rs, plane)

        @pl.when(z > 0)
        def _():
            sums_sent(dn_ss, dn_rs, plane)


    @pl.when(jnp.logical_not(at_top))
    def _():
        low = z < nz // 2
        outer = jnp.logical_or(z == 0, z == nz - 1)
        inner_z = jnp.where(low, 1, nz - 2)
        outer_z = jnp.where(low, 0, nz - 1)

        def lift(src, c, to):
            return remote(src, un_buf.at[c], up_ss.at[0], up_rs.at[c], dev(0, d, to))

        def drop(src, c, to):
            return remote(src, dn_buf.at[c], dn_ss.at[0], dn_rs.at[c], dev(0, d, to))

        def hand_on(block):
            for o in range(1, nz):
                c = block * nz + jnp.where(low, nz - o, o - 1)

                @pl.when(jnp.logical_and(outer, low))
                def _(c=c):
                    lift(p_buf.at[c], c, inner_z).start()

                @pl.when(jnp.logical_and(outer, jnp.logical_not(low)))
                def _(c=c):
                    drop(p_buf.at[c], c, inner_z).start()

            c = block * nz + outer_z

            @pl.when(jnp.logical_and(jnp.logical_not(outer), low))
            def _():
                lift(p_buf.at[c], c, outer_z).start()

            @pl.when(jnp.logical_and(jnp.logical_not(outer), jnp.logical_not(low)))
            def _():
                drop(p_buf.at[c], c, outer_z).start()

        def pass_on(block):
            for o in range(nz // 2):
                to = jnp.where(low, nz - 1 - o, o)
                c = block * nz + to

                @pl.when(jnp.logical_and(jnp.logical_not(outer), low))
                def _(c=c, to=to):
                    lift(p_buf.at[c], c, to).wait_recv()
                    uo_buf[c] = (un_buf[c].astype(F32) + p_buf[c].astype(F32)).astype(BF16)
                    lift(uo_buf.at[c], c, to).start()

                @pl.when(jnp.logical_and(jnp.logical_not(outer), jnp.logical_not(low)))
                def _(c=c, to=to):
                    drop(p_buf.at[c], c, to).wait_recv()
                    uo_buf[c] = (dn_buf[c].astype(F32) + p_buf[c].astype(F32)).astype(BF16)
                    drop(uo_buf.at[c], c, to).start()

        def lower_slope(block):
            c = block * nz + z
            lift(p_buf.at[c], c, z).wait_recv()
            drop(p_buf.at[c], c, z).wait_recv()
            total = p_buf[c].astype(F32) + un_buf[c].astype(F32) + dn_buf[c].astype(F32)
            so_buf[0, block] = slope_of(total).astype(BF16)
            if block:
                so_copy(block).start()
            else:
                slope_copy(0).start()

        def forward(block):
            so_copy(block).wait_recv()
            slope_copy(block).start()

        multiply(0)
        hand_on(0)
        infs_buf[:, :R] = in_features()
        infs_buf[:, R:] = jnp.zeros((tok, lanes - R), BF16)
        for which in range(2):
            side_copy(which).start()
        pl.semaphore_wait(go_sem.at[0], 1)
        a_start()
        pl.semaphore_wait(far_sem.at[0], column - 1)
        pass_on(0)
        for block in range(1, nd):
            a_wait(block)
            multiply(block)
            hand_on(block)
            if block == 1:
                lower_slope(0)
        pass_on(1)
        for block in range(2, nd):
            pass_on(block)
            lower_slope(block - 1)
            if block > 2:
                forward(block - 2)
        lower_slope(nd - 1)
        for block in range(nd - 2, nd):
            forward(block)
        remote(gr_buf, gr_buf, g_ss.at[0], g_rs.at[0], dev(1, d, z)).wait_recv()
        for k in range(SEQS):
            held = gr_buf[k * per_seq * nz]
            for o in range(k * per_seq * nz + 1, (k + 1) * per_seq * nz):
                held = held + gr_buf[o]
            out_ref[k : k + 1, :piece] = held
        score()
        a_sent()
        moved = so_buf.at[0, pl.ds(1, nd - 1)]
        remote(moved, moved, so_ss.at[0], so_rs.at[0], dev(1, d, z)).wait_send()
        slope_arrival().wait_send()
        for which in range(2):
            side_copy(which).wait_send()
        @pl.when(low)
        def _():
            sums_sent(up_ss, up_rs, nd * (nz - 1))

        @pl.when(jnp.logical_not(low))
        def _():
            sums_sent(dn_ss, dn_rs, nd * (nz - 1))

    moved = sc_buf.at[pl.ds(0, column - 1)]
    others = remote(moved, moved, sc_ss.at[0], sc_rs.at[0], dev(1 - s, d, z))
    others.wait_recv()
    scores = sc_buf[0]
    for other in range(1, column):
        scores = scores + sc_buf[other]
    out_ref[:, piece : piece + scores.shape[1]] = scores
    others.wait_send()


def pair_call(nd, nz, tok, width, queries):
    feat, cols, sub, plane, column = width // nz, width // nd, tok // nz, nd * nz, 2 * nz
    piece, lanes = R * R // nz, 2 * R
    dma = pltpu.SemaphoreType.DMA
    sems = []
    for arrivals in (2 * nd - 2, nd - 1, plane, plane, 2 * nd - 2, nd - 1, 1):
        sems += [dma((1,)), dma((arrivals,))]
    sems += [dma((2,)), dma((2,))]
    for _ in range(3):
        sems += [dma((1,)), dma((1,))]
    vmem = pl.BlockSpec(memory_space=pltpu.VMEM)
    hbm = pl.BlockSpec(memory_space=pl.ANY)
    chunks = pltpu.VMEM((plane, sub, cols), BF16)
    blocks = pltpu.VMEM((nd, tok, cols), BF16)
    return pl.pallas_call(
        functools.partial(pair_kernel, nd, nz, LAG, GAP),
        out_shape=pltpu.VMEM((SEQS, piece + queries), F32),
        in_specs=[hbm, hbm, hbm, pl.BlockSpec(memory_space=pltpu.SMEM), hbm, hbm],
        out_specs=vmem,
        scratch_shapes=[
            pltpu.VMEM((tok, width), BF16),
            pltpu.VMEM((feat, cols), BF16),
            pltpu.VMEM((1, width), F32),
            pltpu.VMEM((queries, piece), BF16),
            pltpu.VMEM((cols, feat + lanes), BF16),
            pltpu.VMEM((R, width), BF16),
            pltpu.VMEM((lanes, cols), BF16),
            pltpu.VMEM((tok, feat), F32),
            pltpu.VMEM((tok, 128), F32),
            blocks, chunks, chunks, chunks, chunks, chunks,
            blocks,
            pltpu.VMEM((tok, feat), BF16),
            blocks,
            pltpu.VMEM((nd, tok, lanes), F32),
            pltpu.VMEM((nd, tok, feat + lanes), BF16),
            pltpu.VMEM((nd, tok, feat + lanes), BF16),
            pltpu.VMEM((2, nd, sub, cols), BF16),
            pltpu.VMEM((nz, sub, cols), BF16),
            pltpu.VMEM((lanes, cols), BF16),
            pltpu.VMEM((tok, lanes), BF16),
            pltpu.VMEM((tok, lanes), BF16),
            pltpu.VMEM((tok, cols), BF16),
            pltpu.VMEM((nz + 1, tok, piece), F32),
            pltpu.VMEM((nz, 1, piece), F32),
            pltpu.VMEM((plane, 1, piece), F32),
            pltpu.VMEM((1, piece), F32),
            pltpu.VMEM((nd, 1, piece), F32),
            pltpu.VMEM((column, SEQS, queries), F32),
            pltpu.VMEM((3 * SEQS, piece), F32),
            dma((6,)),
            pltpu.SemaphoreType.REGULAR((1,)),
            pltpu.SemaphoreType.REGULAR((1,)),
            *sems,
        ],
        compiler_params=pltpu.CompilerParams(
            collective_id=0, has_side_effects=True, vmem_limit_bytes=60 * 1024 * 1024
        ),
    )


def stack_call(sections, nd, nz, tok, width, queries):
    feat, cols = width // nz, width // nd
    sub = tok // nz
    piece = R * R // nz
    column = sections * nz
    plane = nd * nz
    vmem = pl.BlockSpec(memory_space=pltpu.VMEM)
    hbm = pl.BlockSpec(memory_space=pl.ANY)
    dma = pltpu.SemaphoreType.DMA
    sems = []
    for shape in ((nd,), (nd,), (nz, nd), (nd,), (nz, nd), (nd,), (plane,)):
        sems += [dma(shape), dma(shape)]
    sems += [dma((nz,)), dma((nd,)), dma((1,)), dma((1,))]
    sems += [dma((plane,)), dma((plane,)), dma((column,)), dma((column,))]
    return pl.pallas_call(
        functools.partial(kernel, sections, nd, nz),
        out_shape=jax.ShapeDtypeStruct((SEQS, piece + queries), F32),
        in_specs=[hbm, hbm, vmem, pl.BlockSpec(memory_space=pltpu.SMEM), hbm, vmem],
        out_specs=vmem,
        scratch_shapes=[
            pltpu.VMEM((nd, tok, feat), BF16),
            pltpu.VMEM((nd, sub, R), F32),
            pltpu.VMEM((nz, nd, sub, cols), BF16),
            pltpu.VMEM((nz, nd, sub, cols), BF16),
            pltpu.VMEM((nd, sub, cols), F32),
            pltpu.VMEM((nd, sub, cols), BF16),
            pltpu.VMEM((tok, feat), BF16),
            pltpu.VMEM((nz, nd, sub, cols), BF16),
            pltpu.VMEM((nd, tok, feat), BF16),
            pltpu.VMEM((nd, tok, feat), BF16),
            pltpu.VMEM((plane, 8, tok), F32),
            pltpu.VMEM((tok, feat), BF16),
            pltpu.VMEM((nz, SEQS, piece), F32),
            pltpu.VMEM((plane, SEQS, piece), F32),
            pltpu.VMEM((column, SEQS, queries), F32),
            pltpu.VMEM((tok, width), BF16),
            pltpu.VMEM((feat, cols), BF16),
            pltpu.VMEM((nd, sub, cols), F32),
            pltpu.VMEM((tok, feat), F32),
            pltpu.VMEM((tok, 128), F32),
            pltpu.VMEM((tok, tok), F32),
            pltpu.VMEM((nz, sub, tok), F32),
            pltpu.VMEM((nz, tok, piece), F32),
            pltpu.VMEM((nz, R, piece), BF16),
            *sems,
            dma((4,)),
            pltpu.SemaphoreType.REGULAR((2,)),
            pltpu.SemaphoreType.REGULAR((1,)),
        ],
        compiler_params=pltpu.CompilerParams(
            collective_id=0, has_side_effects=True, vmem_limit_bytes=60 * 1024 * 1024
        ),
    )


def part_outputs(both_ref, grads_ref, scores_ref):
    piece = grads_ref.shape[1]
    grads_ref[...] = both_ref[:, :piece]
    scores_ref[...] = both_ref[:, piece : piece + scores_ref.shape[1]]


def body(section_input, weights, gains, proj_seeds, out_grad, query_grads):
    sections = lax.axis_size("section")
    nd = lax.axis_size("dp")
    nz = lax.axis_size("tensor")
    tok, width = section_input.shape[1:]
    feat = weights.shape[1]
    cols = weights.shape[2]
    assert nd == nz and feat == cols
    piece = R * R // nz
    queries = query_grads.shape[1]
    vmem = pl.BlockSpec(memory_space=pltpu.VMEM)
    paired = sections == 2 and nd == 4 and nz == 4
    if paired:
        call = pair_call(nd, nz, tok, width, queries)
    else:
        call = stack_call(sections, nd, nz, tok, width, queries)
    out = call(section_input[0], weights[0], gains, proj_seeds, out_grad, query_grads[0])
    if paired:
        out = pltpu.with_memory_space_constraint(out, pltpu.VMEM)
    grads, scores = pl.pallas_call(
        part_outputs,
        out_shape=(
            jax.ShapeDtypeStruct((SEQS, piece), F32),
            jax.ShapeDtypeStruct((SEQS, queries), F32),
        ),
        in_specs=[vmem],
        out_specs=(vmem, vmem),
    )(out)
    return (grads[None], scores)


def solution(mesh):
    in_specs = (
        P("section", "dp", None),
        P("section", "tensor", "dp"),
        P("section", None),
        P("section", None),
        P("dp", None),
        P("section", "dp", "tensor"),
    )
    out_specs = (P("section", None, "tensor"), P(None, "dp"))
    return jax.shard_map(body, mesh=mesh, in_specs=in_specs, out_specs=out_specs, check_vma=False)
```
